128 devices in a mesh: ctx: 16 (over y_lo, x, core), exp: 8 (over y_hi, z).
Axes of the slice: x: 4, y: 4 (y_hi: 2, y_lo: 2; y = y_hi * 2 + y_lo), z: 4, core: 2. Of those that a mesh axis runs over, the one named last changes fastest.
Arguments:
- queries: bfloat16 [2048, 3072], P('ctx', 'exp'), may hold values from -8 to 8
- keys: bfloat16 [2048, 1024], P('ctx', 'exp'), may hold values from -8 to 8
- values: bfloat16 [2048, 1024], P('ctx', 'exp'), may hold values from -6 to 6
- norm_gain: float32 [3072], replicated, may hold values from 0.1 to 1.9
- routes: int32 [2048, 2], P(('ctx', 'exp')), may hold values from 0 to 7, all different within a row; in each aligned block of 16 rows (0 to 15, 16 to 31, ...) at most 6 rows name the same one
- route_scores: float32 [2048, 2], P(('ctx', 'exp')), may hold values from -8 to 8
- cotangent: bfloat16 [2048, 3072], P(('ctx', 'exp')), may hold values from -6 to 6
- w_gate: bfloat16 [8, 3072, 8192], P('exp', None, 'ctx'), may hold values from -0.109375 to 0.109375
- w_up: bfloat16 [8, 3072, 8192], P('exp', None, 'ctx'), may hold values from -0.109375 to 0.109375
- w_down: bfloat16 [8, 8192, 3072], P('exp', 'ctx'), may hold values from -0.0625 to 0.0625
Outputs:
- mixed: bfloat16 [2048, 3072], P(('ctx', 'exp'))
- grad_input: bfloat16 [2048, 3072], P(('ctx', 'exp'))
- grad_gate: bfloat16 [8, 3072, 8192], P('exp', None, 'ctx')
- grad_up: bfloat16 [8, 3072, 8192], P('exp', None, 'ctx')
- grad_down: bfloat16 [8, 8192, 3072], P('exp', 'ctx')
The draws below stay inside these ranges and needn't reach their ends.
Inputs may be any that keep to these rules, and one draw needn't show every extreme that they name: `routes`: each row names two different experts. Within each aligned block of 16 rows (the rows of one device) no expert is named by more than 6 rows, a bound that some block reaches.
All inputs are finite; a program needn't handle non-finite values.
Results may differ from the reference program's by a relative error of at most 0.018.
Values may be sent and summed in bfloat16 or wider, within the bound.
A program may use at most 128 MiB of HBM per device.

```python
import math
import jax
import jax.numpy as jnp
import numpy as np
from jax import lax

HEAD = 128
GROUP = 3
FF = 8192
TOK_DEV = 16
KV_HEADS = 8
Q_HEADS = 24
D = 3072
EXPERTS = 8
CAP = 6
SEQ = 2048
N_CTX = 16


def draw_queries(key, part):
    base = jax.random.normal(jax.random.fold_in(key, 11), (SEQ, Q_HEADS * HEAD), jnp.float32)
    return jnp.clip(base, -6.0, 6.0).astype(jnp.bfloat16)


def draw_keys(key, part):
    base = jax.random.normal(jax.random.fold_in(key, 12), (SEQ, KV_HEADS * HEAD), jnp.float32)
    return jnp.clip(base, -6.0, 6.0).astype(jnp.bfloat16)


def block_scale(stream_key, shape, shards, least, high):
    factor_of = 1.0
    for position, blocks in shards:
        draws = jax.random.uniform(jax.random.fold_in(jax.random.fold_in(stream_key, 6), position), (blocks,), jnp.float32, least / len(shards), high / len(shards))
        factor_of = factor_of * jnp.repeat(jnp.exp(draws), shape[position] // blocks).reshape((-1,) + (1,) * (len(shape) - 1 - position))
    return factor_of


def deal_out(rng, own, number, rows, count, top, reach, skew):
    sequence = jax.random.permutation(rng, count)
    heavy_load, common = load_shares(count, rows * top, reach, skew, True), load_shares(count, rows * top, reach, skew, False)
    places = jnp.arange(count)

    def named(lengths, rotation):
        used = int((lengths > 0).sum())
        fixed = max(1, used // 4)
        shifted = fixed + (places - fixed + rotation * (used - fixed)) % max(1, count - fixed)
        return jnp.zeros((count,), jnp.int32).at[sequence[jnp.where(places < fixed, places, shifted)]].set(jnp.asarray(lengths, jnp.int32))

    lengths = jnp.where(number % 4 == 0, named(heavy_load, number // 4), named(common, number - number // 4 - 1))
    mixed = jax.random.permutation(jax.random.fold_in(own, 3), count)
    giver, sink = mixed[0:count // 2 * 2:2], mixed[1:count // 2 * 2:2]
    slack = jnp.minimum(lengths[giver] - 1, reach - lengths[sink]) // 2
    slack = jnp.where((giver == sequence[0]) | (sink == sequence[0]) | (lengths[sink] == 0), 0, jnp.maximum(slack, 0))
    shifted = jax.random.randint(jax.random.fold_in(own, 4), (count // 2,), 0, 1 << 20) % (slack + 1)
    lengths = lengths.at[giver].add(-shifted).at[sink].add(shifted)
    members = jnp.searchsorted(jnp.cumsum(lengths), jnp.arange(rows * top), side="right").astype(jnp.int32)
    table = members.reshape(top, rows).T
    table = table[jax.random.permutation(jax.random.fold_in(own, 1), rows)]
    rotation = jax.random.randint(jax.random.fold_in(own, 2), (rows, 1), 0, top)
    return jnp.take_along_axis(table, (jnp.arange(top)[None, :] + rotation) % top, axis=1)


def load_shares(amount, total, bound, slope, full):
    loads = [(1 << 20) // math.isqrt(rank ** slope) + 1 for rank in range(1, amount + 1)]
    largest = bound if full else min(bound, max(-(-total // amount), total * loads[0] // sum(loads)))
    least = 1 if total - largest >= amount - 1 else 0
    counts, surplus = [largest] + [least] * (amount - 1), total - largest - least * (amount - 1)
    while surplus > 0:
        candidates = [i for i in range(1, amount) if counts[i] < largest] or [i for i in range(1, amount) if counts[i] < bound]
        pool, left = sum([loads[i] for i in candidates]), surplus
        for i in candidates:
            addition = min(bound - counts[i], max(1, left * loads[i] // pool), surplus)
            counts[i] = counts[i] + addition
            surplus = surplus - addition
    return np.array(counts)


def normal_values(stream_key, shape, width, reach, shards=(), kind=jnp.bfloat16):
    values = width * jax.random.normal(stream_key, shape, jnp.float32)
    if shards:
        values = values * block_scale(stream_key, shape, shards, -0.22, 0.18)
    return jnp.clip(values, -reach, reach).astype(kind)


def setup_inputs(seed: int = 0) -> dict:
    streams_of = jax.random.split(jax.random.key(seed), 11)
    queries = draw_queries(jax.random.fold_in(streams_of[10], 71), 0)
    keys = draw_keys(jax.random.fold_in(streams_of[10], 71), 0)
    values = normal_values(streams_of[2], (SEQ, KV_HEADS * HEAD), 1.0, 6.0, ((0, 16), (1, 8)))
    norm_gain = jnp.clip(1.0 + 0.18 * jax.random.normal(streams_of[3], (D,), jnp.float32), 0.1, 1.9)
    routes_keys = jax.random.split(jax.random.fold_in(streams_of[4], 1), SEQ // TOK_DEV)
    routes_turns = jax.random.permutation(jax.random.fold_in(streams_of[4], 3), SEQ // TOK_DEV)
    routes = jax.vmap(lambda own, number: deal_out(jax.random.fold_in(streams_of[4], 2), own, number, TOK_DEV, EXPERTS, 2, CAP, 2))(routes_keys, routes_turns).reshape((SEQ, 2))
    route_scores = normal_values(streams_of[5], (SEQ, 2), 2.0, 8.0, ((0, 128),), jnp.float32)
    cotangent = normal_values(streams_of[6], (SEQ, D), 1.0, 6.0, ((0, 128),))
    w_gate = normal_values(streams_of[7], (EXPERTS, D, FF), D ** -0.5, 0.109375, ((0, 8), (2, 16)))
    w_up = normal_values(streams_of[8], (EXPERTS, D, FF), D ** -0.5, 0.109375, ((0, 8), (2, 16)))
    w_down = normal_values(streams_of[9], (EXPERTS, FF, D), FF ** -0.5, 0.0625, ((0, 8), (1, 16)))
    return dict(queries=queries, keys=keys, values=values, norm_gain=norm_gain, routes=routes, route_scores=route_scores, cotangent=cotangent, w_gate=w_gate, w_up=w_up, w_down=w_down)


norm_eps = 1e-05
masked_value = -1e+30

def attend_head(inputs):
    query_head, key_head, value_head = inputs
    positions = jnp.arange(SEQ, dtype=jnp.int32)
    allowed = positions[None, :] <= positions[:, None]
    scores = jnp.einsum('sgd,td->gst', query_head, key_head, precision=lax.Precision.HIGHEST) * HEAD ** (-0.5)
    scores = jnp.where(allowed[None, :, :], scores, masked_value)
    largest = lax.optimization_barrier(jnp.max(scores, axis=2))
    weights = jnp.where(allowed[None, :, :], jnp.exp(scores - largest[:, :, None]), 0.0)
    totals = lax.optimization_barrier(jnp.sum(weights, axis=2))
    summed = jnp.einsum('gst,td->sgd', weights, value_head, precision=lax.Precision.HIGHEST)
    return summed / totals.T[:, :, None]

def expert_pass(inputs):
    rows_in, grad_rows, gate_w, up_w, down_w = inputs
    shard = FF // N_CTX
    gate_pre = jnp.dot(rows_in, gate_w, preferred_element_type=jnp.float32)
    up_pre = jnp.dot(rows_in, up_w, preferred_element_type=jnp.float32)
    hidden = (jax.nn.silu(gate_pre) * up_pre).astype(jnp.bfloat16)

    def down_shard(total, index):
        hpart = lax.dynamic_slice_in_dim(hidden, index * shard, shard, 1)
        wpart = lax.dynamic_slice_in_dim(down_w, index * shard, shard, 0)
        term = lax.optimization_barrier(jnp.dot(hpart, wpart, preferred_element_type=jnp.float32).astype(jnp.bfloat16))
        return (total + term.astype(jnp.float32), None)
    shard_ids = jnp.arange(N_CTX, dtype=jnp.int32)
    start_total = jnp.zeros((rows_in.shape[0], D), jnp.float32)
    out_total, _ = lax.scan(down_shard, start_total, shard_ids)
    expert_out = out_total.astype(jnp.bfloat16)
    grad_hidden = lax.dot_general(grad_rows, down_w, (((1,), (1,)), ((), ())), preferred_element_type=jnp.float32)
    grad_down = lax.dot_general(hidden, grad_rows, (((0,), (0,)), ((), ())), preferred_element_type=jnp.float32).astype(jnp.bfloat16)
    sig = jax.nn.sigmoid(gate_pre)
    grad_up_pre = (grad_hidden * (gate_pre * sig)).astype(jnp.bfloat16)
    grad_gate_pre = (grad_hidden * up_pre * sig * (1.0 + gate_pre * (1.0 - sig))).astype(jnp.bfloat16)
    grad_gate = lax.dot_general(rows_in, grad_gate_pre, (((0,), (0,)), ((), ())), preferred_element_type=jnp.float32).astype(jnp.bfloat16)
    grad_upw = lax.dot_general(rows_in, grad_up_pre, (((0,), (0,)), ((), ())), preferred_element_type=jnp.float32).astype(jnp.bfloat16)

    def input_shard(total, index):
        gpart = lax.dynamic_slice_in_dim(grad_gate_pre, index * shard, shard, 1)
        upart = lax.dynamic_slice_in_dim(grad_up_pre, index * shard, shard, 1)
        gw = lax.dynamic_slice_in_dim(gate_w, index * shard, shard, 1)
        uw = lax.dynamic_slice_in_dim(up_w, index * shard, shard, 1)
        term = lax.dot_general(gpart, gw, (((1,), (1,)), ((), ())), preferred_element_type=jnp.float32)
        term = term + lax.dot_general(upart, uw, (((1,), (1,)), ((), ())), preferred_element_type=jnp.float32)
        term = lax.optimization_barrier(term.astype(jnp.bfloat16))
        return (total + term.astype(jnp.float32), None)
    grad_total, _ = lax.scan(input_shard, start_total, shard_ids)
    return (expert_out, grad_total.astype(jnp.bfloat16), grad_gate, grad_upw, grad_down)

def reference(queries, keys, values, norm_gain, routes, route_scores, cotangent, w_gate, w_up, w_down):
    query_all = queries.astype(jnp.float32).reshape(SEQ, KV_HEADS, GROUP, HEAD).transpose(1, 0, 2, 3)
    key_all = keys.astype(jnp.float32).reshape(SEQ, KV_HEADS, HEAD).transpose(1, 0, 2)
    value_all = values.astype(jnp.float32).reshape(SEQ, KV_HEADS, HEAD).transpose(1, 0, 2)
    attended = lax.map(attend_head, (query_all, key_all, value_all))
    attn = attended.transpose(1, 0, 2, 3).reshape(SEQ, D).astype(jnp.bfloat16)
    feats = attn.astype(jnp.float32)
    inv_rms = lax.rsqrt(lax.optimization_barrier(jnp.mean(feats * feats, axis=1)) + norm_eps)
    normed = (feats * inv_rms[:, None] * norm_gain[None, :]).astype(jnp.bfloat16)
    sources = SEQ // TOK_DEV
    block_routes = routes.reshape(sources, 2 * TOK_DEV)
    onehot = (block_routes[:, :, None] == jnp.arange(EXPERTS, dtype=jnp.int32)[None, None, :]).astype(jnp.int32)
    ranks = lax.optimization_barrier(jnp.sum((jnp.cumsum(onehot, axis=1) - onehot) * onehot, axis=2))
    source_ids = jnp.arange(sources, dtype=jnp.int32)[:, None]
    row_index = (source_ids * CAP + ranks).reshape(-1).astype(jnp.int32)
    expert_index = block_routes.reshape(-1).astype(jnp.int32)
    token_index = (jnp.arange(2 * SEQ, dtype=jnp.int32) // 2).astype(jnp.int32)
    rows_all = sources * CAP
    probs = jax.nn.softmax(route_scores, axis=1)
    pair_probs = probs.reshape(-1)
    rows_buffer = jnp.zeros((EXPERTS, rows_all, D), jnp.bfloat16).at[expert_index, row_index].set(normed[token_index])
    grad_pairs = (pair_probs[:, None] * cotangent[token_index].astype(jnp.float32)).astype(jnp.bfloat16)
    grad_buffer = jnp.zeros((EXPERTS, rows_all, D), jnp.bfloat16).at[expert_index, row_index].set(grad_pairs)
    expert_out, grad_rows_in, grad_gate, grad_upw, grad_down = lax.map(expert_pass, (rows_buffer, grad_buffer, w_gate, w_up, w_down))
    picked = expert_out[expert_index, row_index].astype(jnp.float32).reshape(SEQ, 2, D)
    mixed = lax.optimization_barrier(jnp.sum(picked * probs[:, :, None], axis=1)).astype(jnp.bfloat16)
    grad_normed = lax.optimization_barrier(jnp.sum(grad_rows_in[expert_index, row_index].astype(jnp.float32).reshape(SEQ, 2, D), axis=1))
    weighted = grad_normed * norm_gain[None, :]
    inner = lax.optimization_barrier(jnp.mean(weighted * feats, axis=1))
    grad_input = (inv_rms[:, None] * weighted - feats * (inv_rms ** 3 * inner)[:, None]).astype(jnp.bfloat16)
    return (mixed, grad_input, grad_gate, grad_upw, grad_down)
```

```python
import jax
import jax.numpy as jnp
from jax import lax
from jax.sharding import PartitionSpec as P

norm_eps = 1e-05
masked_value = -1e30


def heads_first(query_local, group, head):
    count = query_local.shape[0]
    return query_local.reshape(count, group, head).transpose(1, 0, 2).reshape(group * count, head)


def local(queries, keys, values, norm_gain, routes, route_scores, cotangent, w_gate, w_up, w_down):
    n_exp = lax.axis_size("exp")
    head = keys.shape[1]
    group = queries.shape[1] // head
    tok_ctx = queries.shape[0]
    ctx_index = lax.axis_index("ctx")
    query_flat = heads_first(queries, group, head)
    query_pos = ctx_index * tok_ctx + jnp.tile(jnp.arange(tok_ctx, dtype=jnp.int32), group)
    key_values = lax.all_gather(
        jnp.concatenate([keys, values], axis=1), "ctx", axis=0, tiled=True
    )
    scores = lax.dot_general(
        query_flat, key_values[:, :head], (((1,), (1,)), ((), ())), preferred_element_type=jnp.float32
    ) * head ** (-0.5)
    allowed = jnp.arange(key_values.shape[0], dtype=jnp.int32)[None, :] <= query_pos[:, None]
    scores = jnp.where(allowed, scores, masked_value)
    weights = jnp.exp(scores - jnp.max(scores, axis=1, keepdims=True))
    totals = jnp.sum(weights, axis=1, keepdims=True)
    attended = (
        jnp.dot(
            weights.astype(jnp.bfloat16), key_values[:, head:], preferred_element_type=jnp.float32
        )
        / totals
    )
    attended = (
        attended.reshape(group, tok_ctx, head)
        .transpose(1, 0, 2)
        .reshape(tok_ctx, group * head)
        .astype(jnp.bfloat16)
    )
    features = lax.all_to_all(attended, "exp", split_axis=0, concat_axis=1, tiled=True)
    feats = features.astype(jnp.float32)
    inv_rms = lax.rsqrt(jnp.mean(feats * feats, axis=1) + norm_eps)
    normed = (feats * inv_rms[:, None] * norm_gain[None, :]).astype(jnp.bfloat16)
    tok_dev = normed.shape[0]
    width = normed.shape[1]
    capacity = 3 * tok_dev // n_exp
    slots = n_exp * capacity
    flat_routes = routes.reshape(-1)
    onehot = (flat_routes[:, None] == jnp.arange(n_exp, dtype=jnp.int32)[None, :]).astype(jnp.int32)
    ranks = jnp.sum((jnp.cumsum(onehot, axis=0) - onehot) * onehot, axis=1)
    target = flat_routes * capacity + ranks
    placed = (jnp.arange(slots, dtype=jnp.int32)[:, None] == target[None, :]).astype(jnp.float32)
    place_tokens = placed.reshape(slots, tok_dev, 2).sum(axis=2)
    probs = jax.nn.softmax(route_scores, axis=1)
    mixing = (placed * probs.reshape(-1)[None, :]).reshape(slots, tok_dev, 2).sum(axis=2)
    send = jnp.dot(
        place_tokens.astype(jnp.bfloat16), normed, preferred_element_type=jnp.float32
    ).astype(jnp.bfloat16)
    arrived = lax.all_to_all(
        send.reshape(n_exp, capacity, width), "exp", split_axis=0, concat_axis=0, tiled=True
    ).reshape(slots, width)
    expert_in = lax.all_gather(arrived, "ctx", axis=0, tiled=True)
    gate_w = w_gate[0]
    up_w = w_up[0]
    down_w = w_down[0]
    gate_pre = jnp.dot(expert_in, gate_w, preferred_element_type=jnp.float32)
    up_pre = jnp.dot(expert_in, up_w, preferred_element_type=jnp.float32)
    hidden = (jax.nn.silu(gate_pre) * up_pre).astype(jnp.bfloat16)
    expert_out = lax.psum_scatter(
        jnp.dot(hidden, down_w, preferred_element_type=jnp.float32).astype(jnp.bfloat16),
        "ctx",
        scatter_dimension=0,
        tiled=True,
    )
    returned = lax.all_to_all(
        expert_out.reshape(n_exp, capacity, width), "exp", split_axis=0, concat_axis=0, tiled=True
    ).reshape(slots, width)
    mixed = lax.dot_general(
        mixing,
        returned.astype(jnp.float32),
        (((0,), (0,)), ((), ())),
        precision=lax.Precision.HIGHEST,
    ).astype(jnp.bfloat16)
    grad_slots = jnp.dot(
        mixing, cotangent.astype(jnp.float32), precision=lax.Precision.HIGHEST
    ).astype(jnp.bfloat16)
    grad_arrived = lax.all_to_all(
        grad_slots.reshape(n_exp, capacity, width), "exp", split_axis=0, concat_axis=0, tiled=True
    ).reshape(slots, width)
    grad_out = lax.all_gather(grad_arrived, "ctx", axis=0, tiled=True)
    rows_in = expert_in
    grad_hidden = lax.dot_general(
        grad_out, down_w, (((1,), (1,)), ((), ())), preferred_element_type=jnp.float32
    )
    grad_down = lax.dot_general(
        hidden, grad_out, (((0,), (0,)), ((), ())), preferred_element_type=jnp.float32
    ).astype(jnp.bfloat16)
    sig = jax.nn.sigmoid(gate_pre)
    grad_up_pre = (grad_hidden * (gate_pre * sig)).astype(jnp.bfloat16)
    grad_gate_pre = (grad_hidden * up_pre * sig * (1.0 + gate_pre * (1.0 - sig))).astype(
        jnp.bfloat16
    )
    grad_gate = lax.dot_general(
        rows_in, grad_gate_pre, (((0,), (0,)), ((), ())), preferred_element_type=jnp.float32
    ).astype(jnp.bfloat16)
    grad_upw = lax.dot_general(
        rows_in, grad_up_pre, (((0,), (0,)), ((), ())), preferred_element_type=jnp.float32
    ).astype(jnp.bfloat16)
    term = lax.dot_general(
        grad_gate_pre, gate_w, (((1,), (1,)), ((), ())), preferred_element_type=jnp.float32
    )
    grad_summed = lax.psum_scatter(
        (
            term
            + lax.dot_general(
                grad_up_pre, up_w, (((1,), (1,)), ((), ())), preferred_element_type=jnp.float32
            )
        ).astype(jnp.bfloat16),
        "ctx",
        scatter_dimension=0,
        tiled=True,
    )
    grad_back = lax.all_to_all(
        grad_summed.reshape(n_exp, capacity, width), "exp", split_axis=0, concat_axis=0, tiled=True
    ).reshape(slots, width)
    grad_normed = lax.dot_general(
        place_tokens,
        grad_back.astype(jnp.float32),
        (((0,), (0,)), ((), ())),
        precision=lax.Precision.HIGHEST,
    )
    weighted = grad_normed * norm_gain[None, :]
    inner = jnp.mean(weighted * feats, axis=1)
    grad_input = (inv_rms[:, None] * weighted - feats * (inv_rms**3 * inner)[:, None]).astype(
        jnp.bfloat16
    )
    return (mixed, grad_input, grad_gate[None], grad_upw[None], grad_down[None])


def solution(mesh):
    placed = (
        P("ctx", "exp"),
        P("ctx", "exp"),
        P("ctx", "exp"),
        P(),
        P(("ctx", "exp"), None),
        P(("ctx", "exp"), None),
        P(("ctx", "exp"), None),
        P("exp", None, "ctx"),
        P("exp", None, "ctx"),
        P("exp", "ctx", None),
    )
    return jax.shard_map(
        local,
        mesh=mesh,
        in_specs=placed,
        out_specs=(
            P(("ctx", "exp"), None),
            P(("ctx", "exp"), None),
            P("exp", None, "ctx"),
            P("exp", None, "ctx"),
            P("exp", "ctx", None),
        ),
        check_vma=False,
    )
```

```python
import functools

import jax
import jax.numpy as jnp
from jax import lax
from jax.experimental import pallas as pl
from jax.experimental.pallas import tpu as pltpu
from jax.sharding import PartitionSpec as P

norm_eps = 1e-05
masked_value = -1e30
NX, NY, NC = 4, 2, 2
f32, bf16 = jnp.float32, jnp.bfloat16


class Place:
    def __init__(self):
        c = lax.axis_index("ctx")
        self.k = lax.rem(c, NC)
        self.x = lax.rem(lax.div(c, NC), NX)
        self.y = lax.div(c, NC * NX)
        self.ok = 1 - self.k
        self.oy = 1 - self.y
        self.xr = lax.rem(self.x + 1, NX)
        self.xl = lax.rem(self.x + 3, NX)
        self.xf = lax.rem(self.x + 2, NX)
        self.partner = self.index(self.x, self.y, self.ok)
        self.across = self.index(self.x, self.oy, self.k)
        self.right = self.index(self.xr, self.y, self.k)
        self.left = self.index(self.xl, self.y, self.k)

    def index(self, x, y, k):
        return (y * NX + x) * NC + k


class Copies:
    def __init__(self, send, recv, tensor):
        self.send, self.recv, self.tensor = send, recv, tensor
        self.started, self.count = [], 0

    def start(self, src, dst, device, arrival):
        copy = pltpu.make_async_remote_copy(
            src_ref=src, dst_ref=dst,
            send_sem=self.send.at[self.tensor, self.count],
            recv_sem=self.recv.at[self.tensor, arrival],
            device_id={"ctx": device}, device_id_type=pl.DeviceIdType.MESH,
        )
        copy.start()
        self.started.append(copy)
        self.count += 1

    def arrived(self, ref, arrival, device):
        pltpu.make_async_remote_copy(
            src_ref=ref, dst_ref=ref,
            send_sem=self.send.at[self.tensor, 0],
            recv_sem=self.recv.at[self.tensor, arrival],
            device_id={"ctx": device}, device_id_type=pl.DeviceIdType.MESH,
        ).wait_recv()

    def drain(self):
        for copy in self.started:
            copy.wait_send()


class Gather:
    def __init__(self, copies, buf, rows, width, place):
        self.c, self.buf, self.rows, self.width, self.p = copies, buf, rows, width, place

    def block(self, x, y, k, half=None):
        start = pl.multiple_of(((x * NY + y) * NC + k) * self.rows, 16)
        if half is None:
            return self.buf.at[pl.ds(start, self.rows), :]
        mid = self.width // 2
        return self.buf.at[pl.ds(start, self.rows), pl.ds(half * mid, mid)]

    def send(self, ref, device, arrival):
        self.c.start(ref, ref, device, arrival)

    def own(self):
        p = self.p
        mine = self.block(p.x, p.y, p.k)
        self.send(mine, p.across, 0)
        self.send(mine, p.right, 1)
        self.send(mine, p.left, 2)
        self.send(mine, p.partner, 9)

    def across(self):
        p = self.p
        got = self.block(p.x, p.oy, p.k)
        self.c.arrived(got, 0, p.across)
        self.send(got, p.right, 3)
        self.send(got, p.left, 4)
        self.send(got, p.partner, 10)

    def beside(self, stage):
        p = self.p
        y = p.oy if stage else p.y
        got = self.block(p.xl, y, p.k)
        self.c.arrived(got, 1 + 2 * stage, p.left)
        self.send(self.block(p.xl, y, p.k, 0), p.right, 5 + 2 * stage)
        self.send(got, p.partner, 11 + 2 * stage)
        got = self.block(p.xr, y, p.k)
        self.c.arrived(got, 2 + 2 * stage, p.right)
        self.send(self.block(p.xr, y, p.k, 1), p.left, 6 + 2 * stage)
        self.send(got, p.partner, 12 + 2 * stage)

    def far(self, stage):
        p = self.p
        y = p.oy if stage else p.y
        self.c.arrived(self.block(p.xf, y, p.k, 0), 5 + 2 * stage, p.left)
        self.c.arrived(self.block(p.xf, y, p.k, 1), 6 + 2 * stage, p.right)
        self.send(self.block(p.xf, y, p.k), p.partner, 15 + stage)

    def other_core(self, which):
        p = self.p
        spots = {
            "own": [(p.x, p.y, 9), (p.x, p.oy, 10)],
            "left": [(p.xl, p.y, 11), (p.xl, p.oy, 13)],
            "right": [(p.xr, p.y, 12), (p.xr, p.oy, 14)],
            "far": [(p.xf, p.y, 15), (p.xf, p.oy, 16)],
        }[which]
        for x, y, arrival in spots:
            self.c.arrived(self.block(x, y, p.ok), arrival, p.partner)


def add_into(dst, rows, count, width, first, sources):
    step = 768

    @pl.loop(0, width // step)
    def _(i):
        at = pl.multiple_of(i * step, 128)
        spot = pl.multiple_of(first + i * step, 128)
        total = dst[pl.ds(rows, count), pl.ds(spot, step)].astype(f32)
        for source in sources:
            total = total + source[:, pl.ds(at, step)].astype(f32)
        dst[pl.ds(rows, count), pl.ds(spot, step)] = total.astype(bf16)


class Reduce:
    def __init__(self, copies, buf, core_in, far_in, near_in, across_in, rows, width, place):
        self.c, self.buf, self.p, self.rows, self.width = copies, buf, place, rows, width
        self.core_in, self.far_in, self.near_in, self.across_in = core_in, far_in, near_in, across_in

    def start_of(self, x, y, k):
        return pl.multiple_of(((x * NY + y) * NC + k) * self.rows, 16)

    def block(self, x, y, k):
        return self.buf.at[pl.ds(self.start_of(x, y, k), self.rows), :]

    def half(self, x, y, k, half):
        mid = self.width // 2
        return self.buf.at[pl.ds(self.start_of(x, y, k), self.rows), pl.ds(half * mid, mid)]

    def columns(self):
        p = self.p
        return [p.x, p.xr, p.xl, p.xf]

    def core_send(self, which):
        p = self.p
        x = self.columns()[which]
        for j, y in enumerate((p.oy, p.y)):
            self.c.start(
                self.block(x, y, p.ok), self.core_in.at[which, j], p.partner, which * 2 + j
            )

    def core_add(self, which):
        p = self.p
        x = self.columns()[which]
        for j, y in enumerate((p.oy, p.y)):
            self.c.arrived(self.core_in.at[which, j], which * 2 + j, p.partner)
            add_into(
                self.buf, self.start_of(x, y, p.k), self.rows, self.width, 0,
                [self.core_in.at[which, j]],
            )

    def far_send(self):
        p = self.p
        for j, y in enumerate((p.oy, p.y)):
            self.c.start(self.half(p.xf, y, p.k, 0), self.far_in.at[0, j], p.right, 8 + j)
            self.c.start(self.half(p.xf, y, p.k, 1), self.far_in.at[1, j], p.left, 10 + j)

    def near_send(self):
        p = self.p
        mid = self.width // 2
        for j, y in enumerate((p.oy, p.y)):
            self.c.arrived(self.far_in.at[0, j], 8 + j, p.left)
            add_into(
                self.buf, self.start_of(p.xr, y, p.k), self.rows, mid, 0, [self.far_in.at[0, j]]
            )
            self.c.start(self.block(p.xr, y, p.k), self.near_in.at[0, j], p.right, 12 + j)
            self.c.arrived(self.far_in.at[1, j], 10 + j, p.right)
            add_into(
                self.buf, self.start_of(p.xl, y, p.k), self.rows, mid, mid, [self.far_in.at[1, j]]
            )
            self.c.start(self.block(p.xl, y, p.k), self.near_in.at[1, j], p.left, 14 + j)

    def near_add(self, j):
        p = self.p
        y = (p.oy, p.y)[j]
        self.c.arrived(self.near_in.at[0, j], 12 + j, p.left)
        self.c.arrived(self.near_in.at[1, j], 14 + j, p.right)
        add_into(
            self.buf, self.start_of(p.x, y, p.k), self.rows, self.width, 0,
            [self.near_in.at[0, j], self.near_in.at[1, j]],
        )
        if j == 0:
            self.c.start(self.block(p.x, y, p.k), self.across_in, p.across, 16)

    def finish(self):
        p = self.p
        self.c.arrived(self.across_in, 16, p.across)
        add_into(
            self.buf, self.start_of(p.x, p.y, p.k), self.rows, self.width, 0, [self.across_in]
        )


def dot(a, b, dims=((1,), (0,))):
    return lax.dot_general(a, b, (dims, ((), ())), preferred_element_type=f32)


def expert_kernel(
    rows, width, hidden,
    x_in, dy_in, wg_hbm, wu_hbm, wd_hbm,
    y_out, dx_out, gg_out, gu_out, gd_out,
    xbuf, dybuf, wg, wu, wd, hid, dgb, dub, py, px,
    core_in, far_in, near_in, across_in, gg, gu, gd,
    send, recv, local_sem,
):
    p = Place()
    barrier = pltpu.get_barrier_semaphore()
    for device in (p.partner, p.across, p.right, p.left):
        pl.semaphore_signal(
            barrier, inc=1, device_id={"ctx": device}, device_id_type=pl.DeviceIdType.MESH
        )
    loads = [
        pltpu.make_async_copy(src, dst, local_sem.at[i])
        for i, (src, dst) in enumerate(((wg_hbm, wg), (wu_hbm, wu), (wd_hbm, wd)))
    ]
    gx = Gather(Copies(send, recv, 0), xbuf, rows, width, p)
    gy = Gather(Copies(send, recv, 1), dybuf, rows, width, p)
    first = [
        pltpu.make_async_copy(dy_in, gy.block(p.x, p.y, p.k), local_sem.at[3]),
        pltpu.make_async_copy(x_in, gx.block(p.x, p.y, p.k), local_sem.at[4]),
    ]
    for copy in first + loads:
        copy.start()
    pl.semaphore_wait(barrier, 4)
    first[0].wait()
    gy.own()
    first[1].wait()
    gx.own()
    gy.across()
    gx.across()
    for copy in loads:
        copy.wait()
    col = NY * NC * rows
    tile = 256
    wtile = 512

    def first_half(x):
        at = pl.multiple_of(x * col, 16)

        @pl.loop(0, hidden // tile)
        def _(n):
            cols = pl.ds(pl.multiple_of(n * tile, 128), tile)
            xs = xbuf[pl.ds(at, col), :]
            g = dot(xs, wg[:, cols])
            u = dot(xs, wu[:, cols])
            dh = dot(dybuf[pl.ds(at, col), :], wd[pl.ds(pl.multiple_of(n * tile, 128), tile), :], ((1,), (1,)))
            sig = 1.0 / (1.0 + jnp.exp(-g))
            silu = g * sig
            hid[pl.ds(at, col), cols] = (silu * u).astype(bf16)
            dub[pl.ds(at, col), cols] = (dh * silu).astype(bf16)
            dgb[pl.ds(at, col), cols] = (dh * u * sig * (1.0 + g * (1.0 - sig))).astype(bf16)

    def second_half(x):
        at = pl.multiple_of(x * col, 16)

        @pl.loop(0, width // wtile)
        def _(n):
            spot = pl.ds(pl.multiple_of(n * wtile, 128), wtile)
            py[pl.ds(at, col), spot] = dot(hid[pl.ds(at, col), :], wd[:, spot]).astype(bf16)
            px[pl.ds(at, col), spot] = (
                dot(dgb[pl.ds(at, col), :], wg[spot, :], ((1,), (1,)))
                + dot(dub[pl.ds(at, col), :], wu[spot, :], ((1,), (1,)))
            ).astype(bf16)

    def weight_grads(begin, end):
        @pl.loop(begin, end)
        def _(n):
            spot = pl.ds(pl.multiple_of(n * wtile, 128), wtile)
            gd[:, spot] = dot(hid[...], dybuf[:, spot], ((0,), (0,))).astype(bf16)
            xt = xbuf[:, spot]
            gg[spot, :] = dot(xt, dgb[...], ((0,), (0,))).astype(bf16)
            gu[spot, :] = dot(xt, dub[...], ((0,), (0,))).astype(bf16)
            pltpu.make_async_copy(gd.at[:, spot], gd_out.at[:, spot], local_sem.at[5]).start()
            pltpu.make_async_copy(gg.at[spot, :], gg_out.at[spot, :], local_sem.at[6]).start()
            pltpu.make_async_copy(gu.at[spot, :], gu_out.at[spot, :], local_sem.at[7]).start()

    ry = Reduce(Copies(send, recv, 2), py, core_in.at[0], far_in.at[0], near_in.at[0],
                across_in.at[0], rows, width, p)
    rx = Reduce(Copies(send, recv, 3), px, core_in.at[1], far_in.at[1], near_in.at[1],
                across_in.at[1], rows, width, p)

    def column(which, x):
        first_half(x)
        second_half(x)
        ry.core_send(which)
        rx.core_send(which)

    gy.other_core("own")
    gx.other_core("own")
    gy.beside(0)
    gx.beside(0)
    column(0, p.x)
    gy.beside(1)
    gx.beside(1)
    gy.far(0)
    gx.far(0)
    for side, which, x in (("right", 1, p.xr), ("left", 2, p.xl)):
        gy.other_core(side)
        gx.other_core(side)
        column(which, x)
    gy.far(1)
    gx.far(1)
    gy.other_core("far")
    gx.other_core("far")
    column(3, p.xf)
    ry.core_add(3)
    ry.far_send()
    rx.core_add(3)
    rx.far_send()
    for which in (1, 2, 0):
        ry.core_add(which)
        rx.core_add(which)
    weight_grads(0, 1)
    ry.near_send()
    weight_grads(1, 3)
    rx.near_send()
    weight_grads(3, width // wtile)
    ry.near_add(0)
    ry.near_add(1)
    ry.finish()
    rx.near_add(0)
    rx.near_add(1)
    rx.finish()
    outs = [
        pltpu.make_async_copy(ry.block(p.x, p.y, p.k), y_out, local_sem.at[3]),
        pltpu.make_async_copy(rx.block(p.x, p.y, p.k), dx_out, local_sem.at[4]),
    ]
    for copy in outs:
        copy.start()
    for copy in outs:
        copy.wait()
    pltpu.make_async_copy(gd, gd_out, local_sem.at[5]).wait()
    pltpu.make_async_copy(gg, gg_out, local_sem.at[6]).wait()
    pltpu.make_async_copy(gu, gu_out, local_sem.at[7]).wait()
    for work in (gx, gy, ry, rx):
        work.c.drain()


def experts(x_rows, dy_rows, gate_w, up_w, down_w):
    rows, width = x_rows.shape
    hidden = gate_w.shape[1]
    total = rows * NX * NY * NC

    hbm = pl.BlockSpec(memory_space=pl.ANY)
    return pl.pallas_call(
        functools.partial(expert_kernel, rows, width, hidden),
        out_shape=(
            jax.ShapeDtypeStruct((rows, width), bf16),
            jax.ShapeDtypeStruct((rows, width), bf16),
            jax.ShapeDtypeStruct(gate_w.shape, bf16),
            jax.ShapeDtypeStruct(up_w.shape, bf16),
            jax.ShapeDtypeStruct(down_w.shape, bf16),
        ),
        in_specs=[hbm] * 5,
        out_specs=[hbm] * 5,
        scratch_shapes=[
            pltpu.VMEM((total, width), bf16),
            pltpu.VMEM((total, width), bf16),
            pltpu.VMEM(gate_w.shape, bf16),
            pltpu.VMEM(up_w.shape, bf16),
            pltpu.VMEM(down_w.shape, bf16),
            pltpu.VMEM((total, hidden), bf16),
            pltpu.VMEM((total, hidden), bf16),
            pltpu.VMEM((total, hidden), bf16),
            pltpu.VMEM((total, width), bf16),
            pltpu.VMEM((total, width), bf16),
            pltpu.VMEM((2, 4, 2, rows, width), bf16),
            pltpu.VMEM((2, 2, 2, rows, width // 2), bf16),
            pltpu.VMEM((2, 2, 2, rows, width), bf16),
            pltpu.VMEM((2, rows, width), bf16),
            pltpu.VMEM(gate_w.shape, bf16),
            pltpu.VMEM(up_w.shape, bf16),
            pltpu.VMEM(down_w.shape, bf16),
            pltpu.SemaphoreType.DMA((4, 17)),
            pltpu.SemaphoreType.DMA((4, 17)),
            pltpu.SemaphoreType.DMA((8,)),
        ],
        compiler_params=pltpu.CompilerParams(
            collective_id=0, has_side_effects=True, vmem_limit_bytes=66000000
        ),
        name="experts",
    )(x_rows, dy_rows, gate_w, up_w, down_w)


def heads_first(query_local, group, head):
    count = query_local.shape[0]
    return query_local.reshape(count, group, head).transpose(1, 0, 2).reshape(group * count, head)


def local(queries, keys, values, norm_gain, routes, route_scores, cotangent, w_gate, w_up, w_down):
    n_exp = lax.axis_size("exp")
    head = keys.shape[1]
    group = queries.shape[1] // head
    tok_ctx = queries.shape[0]
    ctx_index = lax.axis_index("ctx")
    query_flat = heads_first(queries, group, head)
    query_pos = ctx_index * tok_ctx + jnp.tile(jnp.arange(tok_ctx, dtype=jnp.int32), group)
    key_values = lax.all_gather(
        jnp.concatenate([keys, values], axis=1), "ctx", axis=0, tiled=True
    )
    scores = lax.dot_general(
        query_flat, key_values[:, :head], (((1,), (1,)), ((), ())), preferred_element_type=jnp.float32
    ) * head ** (-0.5)
    allowed = jnp.arange(key_values.shape[0], dtype=jnp.int32)[None, :] <= query_pos[:, None]
    scores = jnp.where(allowed, scores, masked_value)
    weights = jnp.exp(scores - jnp.max(scores, axis=1, keepdims=True))
    totals = jnp.sum(weights, axis=1, keepdims=True)
    attended = (
        jnp.dot(
            weights.astype(jnp.bfloat16), key_values[:, head:], preferred_element_type=jnp.float32
        )
        / totals
    )
    attended = (
        attended.reshape(group, tok_ctx, head)
        .transpose(1, 0, 2)
        .reshape(tok_ctx, group * head)
        .astype(jnp.bfloat16)
    )
    features = lax.all_to_all(attended, "exp", split_axis=0, concat_axis=1, tiled=True)
    feats = features.astype(jnp.float32)
    inv_rms = lax.rsqrt(jnp.mean(feats * feats, axis=1) + norm_eps)
    normed = (feats * inv_rms[:, None] * norm_gain[None, :]).astype(jnp.bfloat16)
    tok_dev = normed.shape[0]
    width = normed.shape[1]
    capacity = 3 * tok_dev // n_exp
    slots = n_exp * capacity
    flat_routes = routes.reshape(-1)
    onehot = (flat_routes[:, None] == jnp.arange(n_exp, dtype=jnp.int32)[None, :]).astype(jnp.int32)
    ranks = jnp.sum((jnp.cumsum(onehot, axis=0) - onehot) * onehot, axis=1)
    target = flat_routes * capacity + ranks
    placed = (jnp.arange(slots, dtype=jnp.int32)[:, None] == target[None, :]).astype(jnp.float32)
    place_tokens = placed.reshape(slots, tok_dev, 2).sum(axis=2)
    probs = jax.nn.softmax(route_scores, axis=1)
    mixing = (placed * probs.reshape(-1)[None, :]).reshape(slots, tok_dev, 2).sum(axis=2)
    send = jnp.dot(
        place_tokens.astype(jnp.bfloat16), normed, preferred_element_type=jnp.float32
    ).astype(jnp.bfloat16)
    arrived = lax.all_to_all(
        send.reshape(n_exp, capacity, width), "exp", split_axis=0, concat_axis=0, tiled=True
    ).reshape(slots, width)
    grad_slots = jnp.dot(
        mixing, cotangent.astype(jnp.float32), precision=lax.Precision.HIGHEST
    ).astype(jnp.bfloat16)
    grad_arrived = lax.all_to_all(
        grad_slots.reshape(n_exp, capacity, width), "exp", split_axis=0, concat_axis=0, tiled=True
    ).reshape(slots, width)
    expert_out, grad_summed, grad_gate, grad_upw, grad_down = experts(
        arrived, grad_arrived, w_gate[0], w_up[0], w_down[0]
    )
    returned = lax.all_to_all(
        expert_out.reshape(n_exp, capacity, width), "exp", split_axis=0, concat_axis=0, tiled=True
    ).reshape(slots, width)
    mixed = lax.dot_general(
        mixing,
        returned.astype(jnp.float32),
        (((0,), (0,)), ((), ())),
        precision=lax.Precision.HIGHEST,
    ).astype(jnp.bfloat16)
    grad_back = lax.all_to_all(
        grad_summed.reshape(n_exp, capacity, width), "exp", split_axis=0, concat_axis=0, tiled=True
    ).reshape(slots, width)
    grad_normed = lax.dot_general(
        place_tokens,
        grad_back.astype(jnp.float32),
        (((0,), (0,)), ((), ())),
        precision=lax.Precision.HIGHEST,
    )
    weighted = grad_normed * norm_gain[None, :]
    inner = jnp.mean(weighted * feats, axis=1)
    grad_input = (inv_rms[:, None] * weighted - feats * (inv_rms**3 * inner)[:, None]).astype(
        jnp.bfloat16
    )
    return (mixed, grad_input, grad_gate[None], grad_upw[None], grad_down[None])


def solution(mesh):
    placed = (
        P("ctx", "exp"),
        P("ctx", "exp"),
        P("ctx", "exp"),
        P(),
        P(("ctx", "exp"), None),
        P(("ctx", "exp"), None),
        P(("ctx", "exp"), None),
        P("exp", None, "ctx"),
        P("exp", None, "ctx"),
        P("exp", "ctx", None),
    )
    return jax.shard_map(
        local,
        mesh=mesh,
        in_specs=placed,
        out_specs=(
            P(("ctx", "exp"), None),
            P(("ctx", "exp"), None),
            P("exp", None, "ctx"),
            P("exp", None, "ctx"),
            P("exp", "ctx", None),
        ),
        check_vma=False,
    )
```

```python
import functools

import jax
import jax.numpy as jnp
from jax import lax
from jax.experimental import pallas as pl
from jax.experimental.pallas import tpu as pltpu
from jax.sharding import PartitionSpec as P

norm_eps = 1e-05
masked_value = -1e30
NX, NY, NC = 4, 2, 2
f32, bf16 = jnp.float32, jnp.bfloat16


class Place:
    def __init__(self):
        c = lax.axis_index("ctx")
        self.k = lax.rem(c, NC)
        self.x = lax.rem(lax.div(c, NC), NX)
        self.y = lax.div(c, NC * NX)
        self.ok = 1 - self.k
        self.oy = 1 - self.y
        self.xr = lax.rem(self.x + 1, NX)
        self.xl = lax.rem(self.x + 3, NX)
        self.xf = lax.rem(self.x + 2, NX)
        self.partner = self.index(self.x, self.y, self.ok)
        self.across = self.index(self.x, self.oy, self.k)
        self.right = self.index(self.xr, self.y, self.k)
        self.left = self.index(self.xl, self.y, self.k)

    def index(self, x, y, k):
        return (y * NX + x) * NC + k


class Copies:
    def __init__(self, send, recv, tensor, axis="ctx"):
        self.send, self.recv, self.tensor, self.axis = send, recv, tensor, axis
        self.started, self.count = [], 0

    def start(self, src, dst, device, arrival):
        copy = pltpu.make_async_remote_copy(
            src_ref=src, dst_ref=dst,
            send_sem=self.send.at[self.tensor, self.count],
            recv_sem=self.recv.at[self.tensor, arrival],
            device_id={self.axis: device}, device_id_type=pl.DeviceIdType.MESH,
        )
        copy.start()
        self.started.append(copy)
        self.count += 1

    def arrived(self, ref, arrival, device):
        pltpu.make_async_remote_copy(
            src_ref=ref, dst_ref=ref,
            send_sem=self.send.at[self.tensor, 0],
            recv_sem=self.recv.at[self.tensor, arrival],
            device_id={self.axis: device}, device_id_type=pl.DeviceIdType.MESH,
        ).wait_recv()

    def drain(self):
        for copy in self.started:
            copy.wait_send()


class Gather:
    def __init__(self, copies, buf, rows, width, place):
        self.c, self.buf, self.rows, self.width, self.p = copies, buf, rows, width, place

    def block(self, x, y, k, half=None):
        start = pl.multiple_of(((x * NY + y) * NC + k) * self.rows, 16)
        if half is None:
            return self.buf.at[pl.ds(start, self.rows), :]
        mid = self.width // 2
        return self.buf.at[pl.ds(start, self.rows), pl.ds(half * mid, mid)]

    def send(self, ref, device, arrival):
        self.c.start(ref, ref, device, arrival)

    def own(self):
        p = self.p
        mine = self.block(p.x, p.y, p.k)
        self.send(mine, p.across, 0)
        self.send(mine, p.right, 1)
        self.send(mine, p.left, 2)
        self.send(mine, p.partner, 9)

    def across(self):
        p = self.p
        got = self.block(p.x, p.oy, p.k)
        self.c.arrived(got, 0, p.across)
        self.send(got, p.right, 3)
        self.send(got, p.left, 4)
        self.send(got, p.partner, 10)

    def beside(self, stage):
        p = self.p
        y = p.oy if stage else p.y
        got = self.block(p.xl, y, p.k)
        self.c.arrived(got, 1 + 2 * stage, p.left)
        self.send(self.block(p.xl, y, p.k, 0), p.right, 5 + 2 * stage)
        self.send(got, p.partner, 11 + 2 * stage)
        got = self.block(p.xr, y, p.k)
        self.c.arrived(got, 2 + 2 * stage, p.right)
        self.send(self.block(p.xr, y, p.k, 1), p.left, 6 + 2 * stage)
        self.send(got, p.partner, 12 + 2 * stage)

    def far(self, stage):
        p = self.p
        y = p.oy if stage else p.y
        self.c.arrived(self.block(p.xf, y, p.k, 0), 5 + 2 * stage, p.left)
        self.c.arrived(self.block(p.xf, y, p.k, 1), 6 + 2 * stage, p.right)
        self.send(self.block(p.xf, y, p.k), p.partner, 15 + stage)

    def other_core(self, which):
        p = self.p
        spots = {
            "own": [(p.x, p.y, 9), (p.x, p.oy, 10)],
            "left": [(p.xl, p.y, 11), (p.xl, p.oy, 13)],
            "right": [(p.xr, p.y, 12), (p.xr, p.oy, 14)],
            "far": [(p.xf, p.y, 15), (p.xf, p.oy, 16)],
        }[which]
        for x, y, arrival in spots:
            self.c.arrived(self.block(x, y, p.ok), arrival, p.partner)

    def all_but_own(self):
        self.across()
        for stage in range(2):
            self.beside(stage)
        for stage in range(2):
            self.far(stage)
        for which in ("own", "left", "right", "far"):
            self.other_core(which)


def add_into(dst, rows, count, width, first, sources):
    step = 768

    @pl.loop(0, width // step)
    def _(i):
        at = pl.multiple_of(i * step, 128)
        spot = pl.multiple_of(first + i * step, 128)
        total = dst[pl.ds(rows, count), pl.ds(spot, step)].astype(f32)
        for source in sources:
            total = total + source[:, pl.ds(at, step)].astype(f32)
        dst[pl.ds(rows, count), pl.ds(spot, step)] = total.astype(bf16)


class Reduce:
    def __init__(self, copies, buf, core_in, far_in, near_in, across_in, rows, width, place):
        self.c, self.buf, self.p, self.rows, self.width = copies, buf, place, rows, width
        self.core_in, self.far_in, self.near_in, self.across_in = core_in, far_in, near_in, across_in

    def start_of(self, x, y, k):
        return pl.multiple_of(((x * NY + y) * NC + k) * self.rows, 16)

    def block(self, x, y, k):
        return self.buf.at[pl.ds(self.start_of(x, y, k), self.rows), :]

    def half(self, x, y, k, half):
        mid = self.width // 2
        return self.buf.at[pl.ds(self.start_of(x, y, k), self.rows), pl.ds(half * mid, mid)]

    def columns(self):
        p = self.p
        return [p.x, p.xr, p.xl, p.xf]

    def core_send(self, which):
        p = self.p
        x = self.columns()[which]
        for j, y in enumerate((p.oy, p.y)):
            self.c.start(
                self.block(x, y, p.ok), self.core_in.at[which, j], p.partner, which * 2 + j
            )

    def core_add(self, which):
        p = self.p
        x = self.columns()[which]
        for j, y in enumerate((p.oy, p.y)):
            self.c.arrived(self.core_in.at[which, j], which * 2 + j, p.partner)
            add_into(
                self.buf, self.start_of(x, y, p.k), self.rows, self.width, 0,
                [self.core_in.at[which, j]],
            )

    def far_send(self):
        p = self.p
        for j, y in enumerate((p.oy, p.y)):
            self.c.start(self.half(p.xf, y, p.k, 0), self.far_in.at[0, j], p.right, 8 + j)
            self.c.start(self.half(p.xf, y, p.k, 1), self.far_in.at[1, j], p.left, 10 + j)

    def near_send(self):
        p = self.p
        mid = self.width // 2
        for j, y in enumerate((p.oy, p.y)):
            self.c.arrived(self.far_in.at[0, j], 8 + j, p.left)
            add_into(
                self.buf, self.start_of(p.xr, y, p.k), self.rows, mid, 0, [self.far_in.at[0, j]]
            )
            self.c.start(self.block(p.xr, y, p.k), self.near_in.at[0, j], p.right, 12 + j)
            self.c.arrived(self.far_in.at[1, j], 10 + j, p.right)
            add_into(
                self.buf, self.start_of(p.xl, y, p.k), self.rows, mid, mid, [self.far_in.at[1, j]]
            )
            self.c.start(self.block(p.xl, y, p.k), self.near_in.at[1, j], p.left, 14 + j)

    def near_add(self, j):
        p = self.p
        y = (p.oy, p.y)[j]
        self.c.arrived(self.near_in.at[0, j], 12 + j, p.left)
        self.c.arrived(self.near_in.at[1, j], 14 + j, p.right)
        add_into(
            self.buf, self.start_of(p.x, y, p.k), self.rows, self.width, 0,
            [self.near_in.at[0, j], self.near_in.at[1, j]],
        )
        if j == 0:
            self.c.start(self.block(p.x, y, p.k), self.across_in, p.across, 16)

    def finish(self):
        p = self.p
        self.c.arrived(self.across_in, 16, p.across)
        add_into(
            self.buf, self.start_of(p.x, p.y, p.k), self.rows, self.width, 0, [self.across_in]
        )


def dot(a, b, dims=((1,), (0,))):
    return lax.dot_general(a, b, (dims, ((), ())), preferred_element_type=f32)


class HeadGather:
    def __init__(self, copies, buf, head, group, e):
        self.c, self.buf, self.head, self.group = copies, buf, head, group
        hi, z = lax.div(e, 4), lax.rem(e, 4)
        other = 1 - hi
        along = [lax.rem(z + d, 4) for d in (1, 3, 2)]
        self.e = e
        self.mirror = other * 4 + z
        self.peers = [hi * 4 + a for a in along]
        self.mirrors = [other * 4 + a for a in along]

    def block(self, e, h):
        spot = pl.multiple_of((e * self.group + h) * self.head, 128)
        return self.buf.at[:, pl.ds(spot, self.head)]

    def own(self, h):
        mine = self.block(self.e, h)
        self.c.start(mine, mine, self.mirror, h * 7)
        for i, peer in enumerate(self.peers):
            self.c.start(mine, mine, peer, h * 7 + 1 + i)

    def relay(self, h):
        got = self.block(self.mirror, h)
        self.c.arrived(got, h * 7, self.mirror)
        for i, peer in enumerate(self.peers):
            self.c.start(got, got, peer, h * 7 + 4 + i)

    def rest(self, h):
        for i, j in enumerate((1, 0, 2)):
            self.c.arrived(self.block(self.peers[j], h), h * 7 + 1 + i, self.peers[j])
            self.c.arrived(self.block(self.mirrors[j], h), h * 7 + 4 + i, self.peers[j])


class Exchange:
    def __init__(self, copies, out, into, sem, e, n):
        self.c, self.out, self.into, self.e, self.n = copies, out, into, e, n
        self.kept = pltpu.make_async_copy(out.at[e], into.at[e], sem)

    def start(self):
        for d in range(1, self.n):
            peer = lax.rem(self.e + d, self.n)
            self.c.start(self.out.at[peer], self.into.at[self.e], peer, d - 1)
        self.kept.start()

    def finish(self):
        self.kept.wait()
        for d in range(1, self.n):
            peer = lax.rem(self.e + self.n - d, self.n)
            self.c.arrived(self.into.at[peer], d - 1, peer)


def dot(a, b, dims=((1,), (0,))):
    return lax.dot_general(a, b, (dims, ((), ())), preferred_element_type=f32)


def iota(shape, axis):
    return lax.broadcasted_iota(jnp.int32, shape, axis)


def kernel(
    rows, width, hidden, head, group, n_exp,
    q_hbm, k_hbm, v_hbm, gain, routes, scores, cot_hbm, wg_hbm, wu_hbm, wd_hbm,
    mixed_out, gi_out, gg_out, gu_out, gd_out,
    xbuf, dybuf, wg, wu, wd, hid, dgb, dub, dhb, py, px,
    core_in, far_in, near_in, across_in, gg, gu, gd,
    q, kv, attn, cot, slabs_out, slabs_in, spots_out, spots_in, place, mix_hi, mix_lo,
    send, recv, local_sem,
):
    p = Place()
    e = lax.axis_index("exp")
    mesh_id = pl.DeviceIdType.MESH
    tok = q.shape[0]
    tok_dev = cot.shape[0]
    slot = 8
    slots = n_exp * slot
    barrier = pltpu.get_barrier_semaphore()
    for device in (p.partner, p.across, p.right, p.left):
        pl.semaphore_signal(barrier, inc=1, device_id={"ctx": device}, device_id_type=mesh_id)
    for d in range(1, n_exp):
        pl.semaphore_signal(
            barrier, inc=1, device_id={"exp": lax.rem(e + d, n_exp)}, device_id_type=mesh_id
        )

    def copies(tensor, axis="ctx"):
        return Copies(send, recv, tensor, axis)

    gx = Gather(copies(0), xbuf, rows, width, p)
    gy = Gather(copies(1), dybuf, rows, width, p)
    ry = Reduce(copies(2), py, core_in.at[0], far_in.at[0], near_in.at[0],
                across_in.at[0], rows, width, p)
    rx = Reduce(copies(3), px, core_in.at[1], far_in.at[1], near_in.at[1],
                across_in.at[1], rows, width, p)
    gk = Gather(copies(4), kv, tok, 2 * head, p)
    ga = HeadGather(copies(5, "exp"), attn, head, group, e)
    grads_there = Exchange(copies(6, "exp"), slabs_out.at[0], slabs_in.at[0], local_sem.at[8], e, n_exp)
    spots_there = Exchange(copies(7, "exp"), spots_out, spots_in, local_sem.at[9], e, n_exp)
    y_back = Exchange(copies(8, "exp"), slabs_out.at[1], slabs_in.at[1], local_sem.at[10], e, n_exp)
    dx_back = Exchange(copies(9, "exp"), slabs_out.at[2], slabs_in.at[2], local_sem.at[11], e, n_exp)

    own = pl.ds(pl.multiple_of(((p.x * NY + p.y) * NC + p.k) * tok, 16), tok)
    first = [
        pltpu.make_async_copy(k_hbm, kv.at[own, pl.ds(0, head)], local_sem.at[0]),
        pltpu.make_async_copy(v_hbm, kv.at[own, pl.ds(head, head)], local_sem.at[1]),
        pltpu.make_async_copy(cot_hbm, cot, local_sem.at[2]),
        pltpu.make_async_copy(q_hbm, q, local_sem.at[3]),
    ]
    loads = [
        pltpu.make_async_copy(src, dst, local_sem.at[4 + i])
        for i, (src, dst) in enumerate(((wd_hbm, wd), (wg_hbm, wg), (wu_hbm, wu)))
    ]
    for copy in first + loads:
        copy.start()

    lane = iota((tok_dev, slots), 1)
    expert, order = lane >> 3, lane & 7
    in_a = routes[:, 0:1] == expert
    in_b = routes[:, 1:2] == expert
    named = jnp.where(in_a | in_b, 1.0, 0.0)
    earlier = jnp.where(iota((tok_dev, tok_dev), 1) < iota((tok_dev, tok_dev), 0), 1.0, 0.0)
    rank = dot(earlier.astype(bf16), named.astype(bf16))
    here = (named > 0.5) & (rank.astype(jnp.int32) == order)
    top = jnp.max(scores[...], axis=1, keepdims=True)
    odds_a, odds_b = jnp.exp(scores[:, 0:1] - top), jnp.exp(scores[:, 1:2] - top)
    whole = odds_a + odds_b
    mix = jnp.where(here, jnp.where(in_a, odds_a / whole, odds_b / whole), 0.0)
    placed = jnp.where(here, 1.0, 0.0).astype(bf16)
    upper = mix.astype(bf16)
    lower = (mix - upper.astype(f32)).astype(bf16)
    place[...] = placed
    mix_hi[...] = upper
    mix_lo[...] = lower
    shift = jnp.where(
        iota((tok_dev, tok), 1) == iota((tok_dev, tok), 0) + e * tok_dev, 1.0, 0.0
    ).astype(bf16)
    spots_out[...] = dot(placed, shift, ((0,), (0,))).reshape(n_exp, slot, tok)

    pl.semaphore_wait(barrier, 3 + n_exp)
    first[0].wait()
    first[1].wait()
    gk.own()
    spots_there.start()
    first[2].wait()
    chunk = 512

    @pl.loop(0, width // chunk)
    def _(n):
        spot = pl.ds(pl.multiple_of(n * chunk, 128), chunk)
        part = dot(mix_hi[...], cot[:, spot], ((0,), (0,))) + dot(mix_lo[...], cot[:, spot], ((0,), (0,)))
        slabs_out[0, :, :, spot] = part.reshape(n_exp, slot, chunk).astype(bf16)

    grads_there.start()
    row, from_row = iota((rows, slots), 0), iota((rows, slots), 1)
    source = (row * 43) >> 8
    squeeze = jnp.where(from_row == source * slot + (row - source * 6), 1.0, 0.0).astype(bf16)
    gk.across()
    gk.beside(0)
    gk.beside(1)
    gk.far(0)
    gk.far(1)
    spots_there.finish()
    pick = dot(squeeze, spots_in[...].reshape(slots, tok).astype(bf16)).astype(bf16)
    grads_there.finish()
    own_rows = pl.ds(pl.multiple_of(((p.x * NY + p.y) * NC + p.k) * rows, 16), rows)

    @pl.loop(0, width // chunk)
    def _(n):
        spot = pl.ds(pl.multiple_of(n * chunk, 128), chunk)
        slabs = slabs_in[0, :, :, spot].astype(f32).reshape(slots, chunk).astype(bf16)
        dybuf[own_rows, spot] = dot(squeeze, slabs).astype(bf16)

    gy.own()
    first[3].wait()
    for which in ("own", "left", "right", "far"):
        gk.other_core(which)
    total_keys = kv.shape[0]
    at = iota((1, total_keys), 1)
    block = at // tok
    key_pos = (((block >> 1) & 1) * NX * NC + (block >> 2) * NC + (block & 1)) * tok + at % tok
    query_pos = lax.axis_index("ctx") * tok + iota((tok, 1), 0)
    for h in range(group):
        s = dot(q[:, h * head : (h + 1) * head], kv[:, 0:head], ((1,), (1,))) * head ** (-0.5)
        s = jnp.where(key_pos <= query_pos, s, masked_value)
        weights = jnp.exp(s - jnp.max(s, axis=1, keepdims=True))
        total = jnp.sum(weights, axis=1, keepdims=True)
        out = dot(weights.astype(bf16), kv[:, head : 2 * head]) / total
        spot = pl.multiple_of((e * group + h) * head, 128)
        attn[:, pl.ds(spot, head)] = out.astype(bf16)
        ga.own(h)
    for h in range(group):
        ga.relay(h)
    gy.across()
    for h in range(group):
        ga.rest(h)

    def squares(n, total):
        part = attn[:, pl.ds(pl.multiple_of(n * chunk, 128), chunk)].astype(f32)
        return total + jnp.sum(part * part, axis=1, keepdims=True)

    total = lax.fori_loop(0, width // chunk, squares, jnp.zeros((tok, 1), f32))
    inv = lax.rsqrt(total / width + norm_eps)

    @pl.loop(0, width // chunk)
    def _(n):
        spot = pl.ds(pl.multiple_of(n * chunk, 128), chunk)
        normed = (attn[:, spot].astype(f32) * inv * gain[:, spot]).astype(bf16)
        xbuf[own_rows, spot] = dot(pick, normed).astype(bf16)

    gx.own()
    for copy in loads:
        copy.wait()
    col = NY * NC * rows
    tile = 256
    wtile = 512

    def back_half(x):
        at = pl.multiple_of(x * col, 16)

        @pl.loop(0, hidden // tile)
        def _(n):
            spot = pl.ds(pl.multiple_of(n * tile, 128), tile)
            dhb[pl.ds(at, col), spot] = dot(dybuf[pl.ds(at, col), :], wd[spot, :], ((1,), (1,)))

    def first_half(x):
        at = pl.multiple_of(x * col, 16)

        @pl.loop(0, hidden // tile)
        def _(n):
            cols = pl.ds(pl.multiple_of(n * tile, 128), tile)
            xs = xbuf[pl.ds(at, col), :]
            g = dot(xs, wg[:, cols])
            u = dot(xs, wu[:, cols])
            dh = dhb[pl.ds(at, col), cols]
            sig = 1.0 / (1.0 + jnp.exp(-g))
            silu = g * sig
            hid[pl.ds(at, col), cols] = (silu * u).astype(bf16)
            dub[pl.ds(at, col), cols] = (dh * silu).astype(bf16)
            dgb[pl.ds(at, col), cols] = (dh * u * sig * (1.0 + g * (1.0 - sig))).astype(bf16)

    def second_half(x):
        at = pl.multiple_of(x * col, 16)

        @pl.loop(0, width // wtile)
        def _(n):
            spot = pl.ds(pl.multiple_of(n * wtile, 128), wtile)
            py[pl.ds(at, col), spot] = dot(hid[pl.ds(at, col), :], wd[:, spot]).astype(bf16)
            px[pl.ds(at, col), spot] = (
                dot(dgb[pl.ds(at, col), :], wg[spot, :], ((1,), (1,)))
                + dot(dub[pl.ds(at, col), :], wu[spot, :], ((1,), (1,)))
            ).astype(bf16)

    def weight_grads(begin, end):
        @pl.loop(begin, end)
        def _(n):
            spot = pl.ds(pl.multiple_of(n * wtile, 128), wtile)
            gd[:, spot] = dot(hid[...], dybuf[:, spot], ((0,), (0,))).astype(bf16)
            xt = xbuf[:, spot]
            gg[spot, :] = dot(xt, dgb[...], ((0,), (0,))).astype(bf16)
            gu[spot, :] = dot(xt, dub[...], ((0,), (0,))).astype(bf16)
            pltpu.make_async_copy(gd.at[:, spot], gd_out.at[:, spot], local_sem.at[5]).start()
            pltpu.make_async_copy(gg.at[spot, :], gg_out.at[spot, :], local_sem.at[6]).start()
            pltpu.make_async_copy(gu.at[spot, :], gu_out.at[spot, :], local_sem.at[7]).start()

    def column(which, x):
        first_half(x)
        second_half(x)
        ry.core_send(which)
        rx.core_send(which)

    def to_slabs(buf, which):
        row, to_row = iota((slots, rows), 1), iota((slots, rows), 0)
        source = (row * 43) >> 8
        spread = jnp.where(to_row == source * slot + (row - source * 6), 1.0, 0.0).astype(bf16)

        @pl.loop(0, width // chunk)
        def _(n):
            spot = pl.ds(pl.multiple_of(n * chunk, 128), chunk)
            part = dot(spread, buf[own_rows, spot])
            slabs_out[which, :, :, spot] = part.reshape(n_exp, slot, chunk).astype(bf16)

    def from_slabs(which, spot):
        return slabs_in[which, :, :, spot].astype(f32).reshape(slots, chunk).astype(bf16)

    gy.beside(0)
    gy.beside(1)
    gy.other_core("own")
    back_half(p.x)
    gy.far(0)
    gx.across()
    gy.other_core("right")
    gy.other_core("left")
    back_half(p.xr)
    back_half(p.xl)
    gy.far(1)
    gx.beside(0)
    gx.other_core("own")
    column(0, p.x)
    gy.other_core("far")
    back_half(p.xf)
    gx.beside(1)
    gx.other_core("right")
    column(1, p.xr)
    gx.far(0)
    gx.other_core("left")
    column(2, p.xl)
    gx.far(1)
    for which in (1, 2, 0):
        ry.core_add(which)
        rx.core_add(which)
    gx.other_core("far")
    column(3, p.xf)
    ry.core_add(3)
    ry.far_send()
    rx.core_add(3)
    rx.far_send()
    weight_grads(0, 1)
    ry.near_send()
    weight_grads(1, 3)
    rx.near_send()
    weight_grads(3, width // wtile)
    ry.near_add(0)
    ry.near_add(1)
    ry.finish()
    to_slabs(py, 1)
    y_back.start()
    rx.near_add(0)
    y_back.finish()

    @pl.loop(0, width // chunk)
    def _(n):
        spot = pl.ds(pl.multiple_of(n * chunk, 128), chunk)
        slabs = from_slabs(1, spot)
        mixed_out[:, spot] = (dot(mix_hi[...], slabs) + dot(mix_lo[...], slabs)).astype(bf16)

    rx.near_add(1)
    rx.finish()
    to_slabs(px, 2)
    dx_back.start()
    dx_back.finish()
    mine = pl.ds(pl.multiple_of(e * tok_dev, 16), tok_dev)
    feats = attn[mine, :].astype(f32)
    inv_own = lax.rsqrt(jnp.sum(feats * feats, axis=1, keepdims=True) / width + norm_eps)
    back = slabs_in[2].astype(f32).reshape(slots, width).astype(bf16)
    weighted = dot(place[...], back) * gain[...]
    inner = jnp.sum(weighted * feats, axis=1, keepdims=True) / width
    gi_out[...] = (inv_own * weighted - feats * (inv_own * inv_own * inv_own * inner)).astype(bf16)
    pltpu.make_async_copy(gd, gd_out, local_sem.at[5]).wait()
    pltpu.make_async_copy(gg, gg_out, local_sem.at[6]).wait()
    pltpu.make_async_copy(gu, gu_out, local_sem.at[7]).wait()
    for work in (gx, gy, ry, rx, gk, ga, grads_there, spots_there, y_back, dx_back):
        work.c.drain()


def local(queries, keys, values, norm_gain, routes, route_scores, cotangent, w_gate, w_up, w_down):
    n_exp = lax.axis_size("exp")
    head = keys.shape[1]
    group = queries.shape[1] // head
    tok = queries.shape[0]
    tok_dev, width = cotangent.shape
    rows = 3 * tok_dev
    gate_w, up_w, down_w = w_gate[0], w_up[0], w_down[0]
    hidden = gate_w.shape[1]
    total = rows * NX * NY * NC
    slots = 8 * n_exp
    hbm = pl.BlockSpec(memory_space=pl.ANY)
    vmem = pl.BlockSpec(memory_space=pltpu.VMEM)
    mixed, grad_input, grad_gate, grad_upw, grad_down = pl.pallas_call(
        functools.partial(kernel, rows, width, hidden, head, group, n_exp),
        out_shape=(
            jax.ShapeDtypeStruct((tok_dev, width), bf16),
            jax.ShapeDtypeStruct((tok_dev, width), bf16),
            jax.ShapeDtypeStruct(gate_w.shape, bf16),
            jax.ShapeDtypeStruct(up_w.shape, bf16),
            jax.ShapeDtypeStruct(down_w.shape, bf16),
        ),
        in_specs=[hbm, hbm, hbm, vmem, vmem, vmem, hbm, hbm, hbm, hbm],
        out_specs=[vmem, vmem, hbm, hbm, hbm],
        scratch_shapes=[
            pltpu.VMEM((total, width), bf16),
            pltpu.VMEM((total, width), bf16),
            pltpu.VMEM(gate_w.shape, bf16),
            pltpu.VMEM(up_w.shape, bf16),
            pltpu.VMEM(down_w.shape, bf16),
            pltpu.VMEM((total, hidden), bf16),
            pltpu.VMEM((total, hidden), bf16),
            pltpu.VMEM((total, hidden), bf16),
            pltpu.VMEM((total, hidden), f32),
            pltpu.VMEM((total, width), bf16),
            pltpu.VMEM((total, width), bf16),
            pltpu.VMEM((2, 4, 2, rows, width), bf16),
            pltpu.VMEM((2, 2, 2, rows, width // 2), bf16),
            pltpu.VMEM((2, 2, 2, rows, width), bf16),
            pltpu.VMEM((2, rows, width), bf16),
            pltpu.VMEM(gate_w.shape, bf16),
            pltpu.VMEM(up_w.shape, bf16),
            pltpu.VMEM(down_w.shape, bf16),
            pltpu.VMEM(queries.shape, bf16),
            pltpu.VMEM((tok * NX * NY * NC, 2 * head), bf16),
            pltpu.VMEM((tok, width), bf16),
            pltpu.VMEM((tok_dev, width), bf16),
            pltpu.VMEM((3, n_exp, 8, width), bf16),
            pltpu.VMEM((3, n_exp, 8, width), bf16),
            pltpu.VMEM((n_exp, 8, tok), f32),
            pltpu.VMEM((n_exp, 8, tok), f32),
            pltpu.VMEM((tok_dev, slots), bf16),
            pltpu.VMEM((tok_dev, slots), bf16),
            pltpu.VMEM((tok_dev, slots), bf16),
            pltpu.SemaphoreType.DMA((10, 21)),
            pltpu.SemaphoreType.DMA((10, 21)),
            pltpu.SemaphoreType.DMA((12,)),
        ],
        compiler_params=pltpu.CompilerParams(
            collective_id=0, has_side_effects=True, vmem_limit_bytes=67000000
        ),
        name="layer",
    )(
        queries, keys, values, norm_gain.reshape(1, width), routes, route_scores, cotangent,
        gate_w, up_w, down_w,
    )
    return (mixed, grad_input, grad_gate[None], grad_upw[None], grad_down[None])


def solution(mesh):
    placed = (
        P("ctx", "exp"),
        P("ctx", "exp"),
        P("ctx", "exp"),
        P(),
        P(("ctx", "exp"), None),
        P(("ctx", "exp"), None),
        P(("ctx", "exp"), None),
        P("exp", None, "ctx"),
        P("exp", None, "ctx"),
        P("exp", "ctx", None),
    )
    return jax.shard_map(
        local,
        mesh=mesh,
        in_specs=placed,
        out_specs=(
            P(("ctx", "exp"), None),
            P(("ctx", "exp"), None),
            P("exp", None, "ctx"),
            P("exp", None, "ctx"),
            P("exp", "ctx", None),
        ),
        check_vma=False,
    )
```

```python
import functools

import jax
import jax.numpy as jnp
from jax import lax
from jax.experimental import pallas as pl
from jax.experimental.pallas import tpu as pltpu
from jax.sharding import PartitionSpec as P

norm_eps = 1e-05
masked_value = -1e30
NX, NY, NC = 4, 2, 2
f32, bf16 = jnp.float32, jnp.bfloat16


class Place:
    def __init__(self):
        c = lax.axis_index("ctx")
        self.k = lax.rem(c, NC)
        self.x = lax.rem(lax.div(c, NC), NX)
        self.y = lax.div(c, NC * NX)
        self.ok = 1 - self.k
        self.oy = 1 - self.y
        self.xr = lax.rem(self.x + 1, NX)
        self.xl = lax.rem(self.x + 3, NX)
        self.xf = lax.rem(self.x + 2, NX)
        self.partner = self.index(self.x, self.y, self.ok)
        self.across = self.index(self.x, self.oy, self.k)
        self.right = self.index(self.xr, self.y, self.k)
        self.left = self.index(self.xl, self.y, self.k)

    def index(self, x, y, k):
        return (y * NX + x) * NC + k


class Copies:
    def __init__(self, send, recv, tensor, axis="ctx"):
        self.send, self.recv, self.tensor, self.axis = send, recv, tensor, axis
        self.started, self.count = [], 0

    def start(self, src, dst, device, arrival):
        copy = pltpu.make_async_remote_copy(
            src_ref=src, dst_ref=dst,
            send_sem=self.send.at[self.tensor, self.count],
            recv_sem=self.recv.at[self.tensor, arrival],
            device_id={self.axis: device}, device_id_type=pl.DeviceIdType.MESH,
        )
        copy.start()
        self.started.append(copy)
        self.count += 1

    def arrived(self, ref, arrival, device):
        pltpu.make_async_remote_copy(
            src_ref=ref, dst_ref=ref,
            send_sem=self.send.at[self.tensor, 0],
            recv_sem=self.recv.at[self.tensor, arrival],
            device_id={self.axis: device}, device_id_type=pl.DeviceIdType.MESH,
        ).wait_recv()

    def drain(self):
        for copy in self.started:
            copy.wait_send()


class Gather:
    def __init__(self, copies, buf, rows, width, place, over_y=False):
        self.c, self.buf, self.rows, self.width, self.p = copies, buf, rows, width, place
        self.over_y = over_y

    def block(self, x, y, k, half=None):
        start = pl.multiple_of(((x * NY + y) * NC + k) * self.rows, 16)
        if half is None:
            return self.buf.at[pl.ds(start, self.rows), :]
        mid = self.width // 2
        return self.buf.at[pl.ds(start, self.rows), pl.ds(half * mid, mid)]

    def send(self, ref, device, arrival):
        self.c.start(ref, ref, device, arrival)

    def own(self):
        p = self.p
        mine = self.block(p.x, p.y, p.k)
        self.send(mine, p.across, 0)
        self.send(mine, p.right, 1)
        self.send(mine, p.left, 2)
        self.send(mine, p.partner, 9)

    def across(self):
        p = self.p
        got = self.block(p.x, p.oy, p.k)
        self.c.arrived(got, 0, p.across)
        self.send(got, p.right, 3)
        self.send(got, p.left, 4)
        self.send(got, p.partner, 10)

    def beside(self, stage):
        p = self.p
        y = p.oy if stage else p.y
        got = self.block(p.xl, y, p.k)
        self.c.arrived(got, 1 + 2 * stage, p.left)
        if not (stage and self.over_y):
            self.send(self.block(p.xl, y, p.k, 0), p.right, 5 + 2 * stage)
        self.send(got, p.partner, 11 + 2 * stage)
        got = self.block(p.xr, y, p.k)
        self.c.arrived(got, 2 + 2 * stage, p.right)
        if not (stage and self.over_y):
            self.send(self.block(p.xr, y, p.k, 1), p.left, 6 + 2 * stage)
        self.send(got, p.partner, 12 + 2 * stage)

    def far(self, stage):
        p = self.p
        y = p.oy if stage else p.y
        if stage and self.over_y:
            self.c.arrived(self.block(p.xf, y, p.k), 7, p.across)
        else:
            self.c.arrived(self.block(p.xf, y, p.k, 0), 5 + 2 * stage, p.left)
            self.c.arrived(self.block(p.xf, y, p.k, 1), 6 + 2 * stage, p.right)
        if self.over_y and not stage:
            self.send(self.block(p.xf, y, p.k), p.across, 7)
        self.send(self.block(p.xf, y, p.k), p.partner, 15 + stage)

    def other_core(self, which):
        p = self.p
        spots = {
            "own": [(p.x, p.y, 9), (p.x, p.oy, 10)],
            "left": [(p.xl, p.y, 11), (p.xl, p.oy, 13)],
            "right": [(p.xr, p.y, 12), (p.xr, p.oy, 14)],
            "far": [(p.xf, p.y, 15), (p.xf, p.oy, 16)],
        }[which]
        for x, y, arrival in spots:
            self.c.arrived(self.block(x, y, p.ok), arrival, p.partner)

    def all_but_own(self):
        self.across()
        for stage in range(2):
            self.beside(stage)
        for stage in range(2):
            self.far(stage)
        for which in ("own", "left", "right", "far"):
            self.other_core(which)


def add_into(dst, rows, count, width, first, sources):
    step = 768

    @pl.loop(0, width // step)
    def _(i):
        at = pl.multiple_of(i * step, 128)
        spot = pl.multiple_of(first + i * step, 128)
        total = dst[pl.ds(rows, count), pl.ds(spot, step)].astype(f32)
        for source in sources:
            total = total + source[:, pl.ds(at, step)].astype(f32)
        dst[pl.ds(rows, count), pl.ds(spot, step)] = total.astype(bf16)


class Reduce:
    def __init__(
        self, copies, buf, core_in, far_in, near_in, across_in, far_across_in, rows, width, place
    ):
        self.c, self.buf, self.p, self.rows, self.width = copies, buf, place, rows, width
        self.core_in, self.far_in, self.near_in, self.across_in = core_in, far_in, near_in, across_in
        self.far_across_in = far_across_in

    def start_of(self, x, y, k):
        return pl.multiple_of(((x * NY + y) * NC + k) * self.rows, 16)

    def block(self, x, y, k):
        return self.buf.at[pl.ds(self.start_of(x, y, k), self.rows), :]

    def half(self, x, y, k, half):
        mid = self.width // 2
        return self.buf.at[pl.ds(self.start_of(x, y, k), self.rows), pl.ds(half * mid, mid)]

    def columns(self):
        p = self.p
        return [p.x, p.xr, p.xl, p.xf]

    def core_send(self, which):
        p = self.p
        x = self.columns()[which]
        for j, y in enumerate((p.oy, p.y)):
            self.c.start(
                self.block(x, y, p.ok), self.core_in.at[which, j], p.partner, which * 2 + j
            )

    def core_add(self, which):
        p = self.p
        x = self.columns()[which]
        for j, y in enumerate((p.oy, p.y)):
            self.c.arrived(self.core_in.at[which, j], which * 2 + j, p.partner)
            add_into(
                self.buf, self.start_of(x, y, p.k), self.rows, self.width, 0,
                [self.core_in.at[which, j]],
            )

    def near_early(self, side):
        p = self.p
        x, device = ((p.xr, p.right), (p.xl, p.left))[side]
        self.c.start(self.block(x, p.oy, p.k), self.near_in.at[side, 0], device, 12 + 2 * side)

    def far_across(self):
        p = self.p
        self.c.start(self.block(p.xf, p.oy, p.k), self.far_across_in, p.across, 17)

    def far_send(self):
        p = self.p
        self.c.arrived(self.far_across_in, 17, p.across)
        add_into(
            self.buf, self.start_of(p.xf, p.y, p.k), self.rows, self.width, 0, [self.far_across_in]
        )
        self.c.start(self.half(p.xf, p.y, p.k, 0), self.far_in.at[0], p.right, 8)
        self.c.start(self.half(p.xf, p.y, p.k, 1), self.far_in.at[1], p.left, 9)

    def near_send(self):
        p = self.p
        mid = self.width // 2
        self.c.arrived(self.far_in.at[0], 8, p.left)
        add_into(self.buf, self.start_of(p.xr, p.y, p.k), self.rows, mid, 0, [self.far_in.at[0]])
        self.c.start(self.block(p.xr, p.y, p.k), self.near_in.at[0, 1], p.right, 13)
        self.c.arrived(self.far_in.at[1], 9, p.right)
        add_into(self.buf, self.start_of(p.xl, p.y, p.k), self.rows, mid, mid, [self.far_in.at[1]])
        self.c.start(self.block(p.xl, p.y, p.k), self.near_in.at[1, 1], p.left, 15)

    def near_add(self, j):
        p = self.p
        y = (p.oy, p.y)[j]
        self.c.arrived(self.near_in.at[0, j], 12 + j, p.left)
        self.c.arrived(self.near_in.at[1, j], 14 + j, p.right)
        add_into(
            self.buf, self.start_of(p.x, y, p.k), self.rows, self.width, 0,
            [self.near_in.at[0, j], self.near_in.at[1, j]],
        )
        if j == 0:
            self.c.start(self.block(p.x, y, p.k), self.across_in, p.across, 16)

    def finish(self):
        p = self.p
        self.c.arrived(self.across_in, 16, p.across)
        add_into(
            self.buf, self.start_of(p.x, p.y, p.k), self.rows, self.width, 0, [self.across_in]
        )


def dot(a, b, dims=((1,), (0,))):
    return lax.dot_general(a, b, (dims, ((), ())), preferred_element_type=f32)


class HeadGather:
    def __init__(self, copies, buf, head, group, e):
        self.c, self.buf, self.head, self.group = copies, buf, head, group
        hi, z = lax.div(e, 4), lax.rem(e, 4)
        up, down, far = [lax.rem(z + d, 4) for d in (1, 3, 2)]
        self.e = e
        self.mirror = (1 - hi) * 4 + z
        self.up, self.down = hi * 4 + up, hi * 4 + down
        self.ups = [self.up, (1 - hi) * 4 + up]
        self.downs = [self.down, (1 - hi) * 4 + down]
        self.fars = [hi * 4 + far, (1 - hi) * 4 + far]

    def block(self, e, h, half=None):
        spot = pl.multiple_of((e * self.group + h) * self.head, 128)
        if half is None:
            return self.buf.at[:, pl.ds(spot, self.head)]
        count = self.buf.shape[0] // 2
        return self.buf.at[pl.ds(half * count, count), pl.ds(spot, self.head)]

    def own(self, h):
        mine = self.block(self.e, h)
        self.c.start(mine, mine, self.mirror, h * 9)
        self.c.start(mine, mine, self.up, h * 9 + 1)
        self.c.start(mine, mine, self.down, h * 9 + 2)

    def relay(self, h):
        got = self.block(self.mirror, h)
        self.c.arrived(got, h * 9, self.mirror)
        self.c.start(got, got, self.up, h * 9 + 3)
        self.c.start(got, got, self.down, h * 9 + 4)

    def forward(self, h):
        for i in range(2):
            self.c.arrived(self.block(self.downs[i], h), h * 9 + 1 + 2 * i, self.down)
            part = self.block(self.downs[i], h, 0)
            self.c.start(part, part, self.up, h * 9 + 5 + 2 * i)
            self.c.arrived(self.block(self.ups[i], h), h * 9 + 2 + 2 * i, self.up)
            part = self.block(self.ups[i], h, 1)
            self.c.start(part, part, self.down, h * 9 + 6 + 2 * i)

    def rest(self, h):
        for i in range(2):
            self.c.arrived(self.block(self.fars[i], h, 0), h * 9 + 5 + 2 * i, self.down)
            self.c.arrived(self.block(self.fars[i], h, 1), h * 9 + 6 + 2 * i, self.up)


class Exchange:
    def __init__(self, copies, out, into, sem, e, n):
        self.c, self.out, self.into, self.e, self.n = copies, out, into, e, n
        self.kept = pltpu.make_async_copy(out.at[e], into.at[e], sem)

    def start(self):
        for d in range(1, self.n):
            peer = lax.rem(self.e + d, self.n)
            self.c.start(self.out.at[peer], self.into.at[self.e], peer, d - 1)
        self.kept.start()

    def finish(self):
        self.kept.wait()
        for d in range(1, self.n):
            peer = lax.rem(self.e + self.n - d, self.n)
            self.c.arrived(self.into.at[peer], d - 1, peer)


def dot(a, b, dims=((1,), (0,))):
    return lax.dot_general(a, b, (dims, ((), ())), preferred_element_type=f32)


def iota(shape, axis):
    return lax.broadcasted_iota(jnp.int32, shape, axis)


def kernel(
    rows, width, hidden, head, group, n_exp,
    q_hbm, k_hbm, v_hbm, gain, routes, scores, cot_hbm, wg_hbm, wu_hbm, wd_hbm,
    mixed_out, gi_out, gg_out, gu_out, gd_out,
    xbuf, dybuf, wg, wu, wd, hid, dgb, dub, dhb, py, px,
    core_in, far_in, near_in, across_in, far_across_in, gg, gu, gd,
    q, kv, attn, cot, slabs_out, slabs_in, spots_out, spots_in, place, mix_hi, mix_lo,
    send, recv, local_sem,
):
    p = Place()
    e = lax.axis_index("exp")
    mesh_id = pl.DeviceIdType.MESH
    tok = q.shape[0]
    tok_dev = cot.shape[0]
    slot = 8
    slots = n_exp * slot
    barrier = pltpu.get_barrier_semaphore()
    for device in (p.partner, p.across, p.right, p.left):
        pl.semaphore_signal(barrier, inc=1, device_id={"ctx": device}, device_id_type=mesh_id)
    for d in range(1, n_exp):
        pl.semaphore_signal(
            barrier, inc=1, device_id={"exp": lax.rem(e + d, n_exp)}, device_id_type=mesh_id
        )

    def copies(tensor, axis="ctx"):
        return Copies(send, recv, tensor, axis)

    gx = Gather(copies(0), xbuf, rows, width, p, True)
    gy = Gather(copies(1), dybuf, rows, width, p, True)
    ry = Reduce(copies(2), py, core_in.at[0], far_in.at[0], near_in.at[0],
                across_in.at[0], far_across_in.at[0], rows, width, p)
    rx = Reduce(copies(3), px, core_in.at[1], far_in.at[1], near_in.at[1],
                across_in.at[1], far_across_in.at[1], rows, width, p)
    gk = Gather(copies(4), kv, tok, 2 * head, p)
    ga = HeadGather(copies(5, "exp"), attn, head, group, e)
    grads_there = Exchange(copies(6, "exp"), slabs_out.at[0], slabs_in.at[0], local_sem.at[8], e, n_exp)
    spots_there = Exchange(copies(7, "exp"), spots_out, spots_in, local_sem.at[9], e, n_exp)
    y_back = Exchange(copies(8, "exp"), slabs_out.at[1], slabs_in.at[1], local_sem.at[10], e, n_exp)
    dx_back = Exchange(copies(9, "exp"), slabs_out.at[2], slabs_in.at[2], local_sem.at[11], e, n_exp)

    own = pl.ds(pl.multiple_of(((p.x * NY + p.y) * NC + p.k) * tok, 16), tok)
    first = [
        pltpu.make_async_copy(k_hbm, kv.at[own, pl.ds(0, head)], local_sem.at[0]),
        pltpu.make_async_copy(v_hbm, kv.at[own, pl.ds(head, head)], local_sem.at[1]),
        pltpu.make_async_copy(cot_hbm, cot, local_sem.at[2]),
        pltpu.make_async_copy(q_hbm, q, local_sem.at[3]),
    ]
    loads = [
        pltpu.make_async_copy(src, dst, local_sem.at[4 + i])
        for i, (src, dst) in enumerate(((wd_hbm, wd), (wg_hbm, wg), (wu_hbm, wu)))
    ]
    for copy in first + loads:
        copy.start()

    lane = iota((tok_dev, slots), 1)
    expert, order = lane >> 3, lane & 7
    in_a = routes[:, 0:1] == expert
    in_b = routes[:, 1:2] == expert
    named = jnp.where(in_a | in_b, 1.0, 0.0)
    earlier = jnp.where(iota((tok_dev, tok_dev), 1) < iota((tok_dev, tok_dev), 0), 1.0, 0.0)
    rank = dot(earlier.astype(bf16), named.astype(bf16))
    here = (named > 0.5) & (rank.astype(jnp.int32) == order)
    top = jnp.max(scores[...], axis=1, keepdims=True)
    odds_a, odds_b = jnp.exp(scores[:, 0:1] - top), jnp.exp(scores[:, 1:2] - top)
    whole = odds_a + odds_b
    mix = jnp.where(here, jnp.where(in_a, odds_a / whole, odds_b / whole), 0.0)
    placed = jnp.where(here, 1.0, 0.0).astype(bf16)
    upper = mix.astype(bf16)
    lower = (mix - upper.astype(f32)).astype(bf16)
    place[...] = placed
    mix_hi[...] = upper
    mix_lo[...] = lower
    shift = jnp.where(
        iota((tok_dev, tok), 1) == iota((tok_dev, tok), 0) + e * tok_dev, 1.0, 0.0
    ).astype(bf16)
    spots_out[...] = dot(placed, shift, ((0,), (0,))).reshape(n_exp, slot, tok)

    pl.semaphore_wait(barrier, 3 + n_exp)
    first[0].wait()
    first[1].wait()
    gk.own()
    spots_there.start()
    first[2].wait()
    chunk = 512

    @pl.loop(0, width // chunk)
    def _(n):
        spot = pl.ds(pl.multiple_of(n * chunk, 128), chunk)
        part = dot(mix_hi[...], cot[:, spot], ((0,), (0,))) + dot(mix_lo[...], cot[:, spot], ((0,), (0,)))
        slabs_out[0, :, :, spot] = part.reshape(n_exp, slot, chunk).astype(bf16)

    grads_there.start()
    row, from_row = iota((rows, slots), 0), iota((rows, slots), 1)
    source = (row * 43) >> 8
    squeeze = jnp.where(from_row == source * slot + (row - source * 6), 1.0, 0.0).astype(bf16)
    gk.across()
    gk.beside(0)
    gk.beside(1)
    gk.far(0)
    gk.far(1)
    spots_there.finish()
    pick = dot(squeeze, spots_in[...].reshape(slots, tok).astype(bf16)).astype(bf16)
    grads_there.finish()
    own_rows = pl.ds(pl.multiple_of(((p.x * NY + p.y) * NC + p.k) * rows, 16), rows)

    @pl.loop(0, width // chunk)
    def _(n):
        spot = pl.ds(pl.multiple_of(n * chunk, 128), chunk)
        slabs = slabs_in[0, :, :, spot].astype(f32).reshape(slots, chunk).astype(bf16)
        dybuf[own_rows, spot] = dot(squeeze, slabs).astype(bf16)

    gy.own()
    first[3].wait()
    for which in ("own", "left", "right", "far"):
        gk.other_core(which)
    total_keys = kv.shape[0]
    at = iota((1, total_keys), 1)
    block = at // tok
    key_pos = (((block >> 1) & 1) * NX * NC + (block >> 2) * NC + (block & 1)) * tok + at % tok
    query_pos = lax.axis_index("ctx") * tok + iota((tok, 1), 0)
    for h in range(group):
        s = dot(q[:, h * head : (h + 1) * head], kv[:, 0:head], ((1,), (1,))) * head ** (-0.5)
        s = jnp.where(key_pos <= query_pos, s, masked_value)
        weights = jnp.exp(s - jnp.max(s, axis=1, keepdims=True))
        total = jnp.sum(weights, axis=1, keepdims=True)
        out = dot(weights.astype(bf16), kv[:, head : 2 * head]) / total
        spot = pl.multiple_of((e * group + h) * head, 128)
        attn[:, pl.ds(spot, head)] = out.astype(bf16)
        ga.own(h)
    for h in range(group):
        ga.relay(h)
    gy.beside(0)
    gy.across()
    for h in range(group):
        ga.forward(h)
    for h in range(group):
        ga.rest(h)
    gy.far(0)

    def squares(n, total):
        part = attn[:, pl.ds(pl.multiple_of(n * chunk, 128), chunk)].astype(f32)
        return total + jnp.sum(part * part, axis=1, keepdims=True)

    total = lax.fori_loop(0, width // chunk, squares, jnp.zeros((tok, 1), f32))
    inv = lax.rsqrt(total / width + norm_eps)

    @pl.loop(0, width // chunk)
    def _(n):
        spot = pl.ds(pl.multiple_of(n * chunk, 128), chunk)
        normed = (attn[:, spot].astype(f32) * inv * gain[:, spot]).astype(bf16)
        xbuf[own_rows, spot] = dot(pick, normed).astype(bf16)

    gx.own()
    for copy in loads:
        copy.wait()
    col = NY * NC * rows
    tile = 256
    wtile = 512

    def back_half(x):
        at = pl.multiple_of(x * col, 16)

        @pl.loop(0, hidden // tile)
        def _(n):
            spot = pl.ds(pl.multiple_of(n * tile, 128), tile)
            dhb[pl.ds(at, col), spot] = dot(dybuf[pl.ds(at, col), :], wd[spot, :], ((1,), (1,)))

    def first_half(x):
        at = pl.multiple_of(x * col, 16)

        @pl.loop(0, hidden // tile)
        def _(n):
            cols = pl.ds(pl.multiple_of(n * tile, 128), tile)
            xs = xbuf[pl.ds(at, col), :]
            g = dot(xs, wg[:, cols])
            u = dot(xs, wu[:, cols])
            dh = dhb[pl.ds(at, col), cols]
            sig = 1.0 / (1.0 + jnp.exp(-g))
            silu = g * sig
            hid[pl.ds(at, col), cols] = (silu * u).astype(bf16)
            dub[pl.ds(at, col), cols] = (dh * silu).astype(bf16)
            dgb[pl.ds(at, col), cols] = (dh * u * sig * (1.0 + g * (1.0 - sig))).astype(bf16)

    def expert_out(x):
        at = pl.multiple_of(x * col, 16)

        @pl.loop(0, width // wtile)
        def _(n):
            spot = pl.ds(pl.multiple_of(n * wtile, 128), wtile)
            py[pl.ds(at, col), spot] = dot(hid[pl.ds(at, col), :], wd[:, spot]).astype(bf16)

    def input_grad(x):
        at = pl.multiple_of(x * col, 16)

        @pl.loop(0, width // wtile)
        def _(n):
            spot = pl.ds(pl.multiple_of(n * wtile, 128), wtile)
            px[pl.ds(at, col), spot] = (
                dot(dgb[pl.ds(at, col), :], wg[spot, :], ((1,), (1,)))
                + dot(dub[pl.ds(at, col), :], wu[spot, :], ((1,), (1,)))
            ).astype(bf16)

    def weight_grads(begin, end):
        @pl.loop(begin, end)
        def _(n):
            spot = pl.ds(pl.multiple_of(n * wtile, 128), wtile)
            gd[:, spot] = dot(hid[...], dybuf[:, spot], ((0,), (0,))).astype(bf16)
            xt = xbuf[:, spot]
            gg[spot, :] = dot(xt, dgb[...], ((0,), (0,))).astype(bf16)
            gu[spot, :] = dot(xt, dub[...], ((0,), (0,))).astype(bf16)
            pltpu.make_async_copy(gd.at[:, spot], gd_out.at[:, spot], local_sem.at[5]).start()
            pltpu.make_async_copy(gg.at[spot, :], gg_out.at[spot, :], local_sem.at[6]).start()
            pltpu.make_async_copy(gu.at[spot, :], gu_out.at[spot, :], local_sem.at[7]).start()

    def rest_of_column(which, x):
        expert_out(x)
        ry.core_send(which)
        input_grad(x)
        rx.core_send(which)

    def near_early(which):
        for work in (ry, rx):
            work.core_add(which)
            work.near_early(which - 1)

    def to_slabs(buf, which):
        row, to_row = iota((slots, rows), 1), iota((slots, rows), 0)
        source = (row * 43) >> 8
        spread = jnp.where(to_row == source * slot + (row - source * 6), 1.0, 0.0).astype(bf16)

        @pl.loop(0, width // chunk)
        def _(n):
            spot = pl.ds(pl.multiple_of(n * chunk, 128), chunk)
            part = dot(spread, buf[own_rows, spot])
            slabs_out[which, :, :, spot] = part.reshape(n_exp, slot, chunk).astype(bf16)

    def from_slabs(which, spot):
        return slabs_in[which, :, :, spot].astype(f32).reshape(slots, chunk).astype(bf16)

    gy.beside(1)
    gy.other_core("own")
    back_half(p.x)
    gy.other_core("right")
    gy.other_core("left")
    back_half(p.xr)
    back_half(p.xl)
    gy.far(1)
    gx.beside(0)
    gx.across()
    gx.other_core("own")
    first_half(p.x)
    rest_of_column(0, p.x)
    gx.far(0)
    gy.other_core("far")
    back_half(p.xf)
    gx.beside(1)
    gx.other_core("right")
    first_half(p.xr)
    rest_of_column(1, p.xr)
    gx.other_core("left")
    first_half(p.xl)
    near_early(1)
    rest_of_column(2, p.xl)
    gx.far(1)
    gx.other_core("far")
    first_half(p.xf)
    near_early(2)
    rest_of_column(3, p.xf)
    ry.core_add(3)
    ry.far_across()
    rx.core_add(3)
    rx.far_across()
    ry.core_add(0)
    rx.core_add(0)
    weight_grads(0, 2)
    ry.far_send()
    ry.near_add(0)
    weight_grads(2, 3)
    rx.far_send()
    rx.near_add(0)
    weight_grads(3, 4)
    ry.near_send()
    weight_grads(4, 5)
    rx.near_send()
    weight_grads(5, width // wtile)
    ry.near_add(1)
    ry.finish()
    to_slabs(py, 1)
    y_back.start()
    rx.near_add(1)
    rx.finish()
    to_slabs(px, 2)
    dx_back.start()
    y_back.finish()

    @pl.loop(0, width // chunk)
    def _(n):
        spot = pl.ds(pl.multiple_of(n * chunk, 128), chunk)
        slabs = from_slabs(1, spot)
        mixed_out[:, spot] = (dot(mix_hi[...], slabs) + dot(mix_lo[...], slabs)).astype(bf16)

    dx_back.finish()
    mine = pl.ds(pl.multiple_of(e * tok_dev, 16), tok_dev)
    feats = attn[mine, :].astype(f32)
    inv_own = lax.rsqrt(jnp.sum(feats * feats, axis=1, keepdims=True) / width + norm_eps)
    back = slabs_in[2].astype(f32).reshape(slots, width).astype(bf16)
    weighted = dot(place[...], back) * gain[...]
    inner = jnp.sum(weighted * feats, axis=1, keepdims=True) / width
    gi_out[...] = (inv_own * weighted - feats * (inv_own * inv_own * inv_own * inner)).astype(bf16)
    pltpu.make_async_copy(gd, gd_out, local_sem.at[5]).wait()
    pltpu.make_async_copy(gg, gg_out, local_sem.at[6]).wait()
    pltpu.make_async_copy(gu, gu_out, local_sem.at[7]).wait()
    for work in (gx, gy, ry, rx, gk, ga, grads_there, spots_there, y_back, dx_back):
        work.c.drain()


def local(queries, keys, values, norm_gain, routes, route_scores, cotangent, w_gate, w_up, w_down):
    n_exp = lax.axis_size("exp")
    head = keys.shape[1]
    group = queries.shape[1] // head
    tok = queries.shape[0]
    tok_dev, width = cotangent.shape
    rows = 3 * tok_dev
    gate_w, up_w, down_w = w_gate[0], w_up[0], w_down[0]
    hidden = gate_w.shape[1]
    total = rows * NX * NY * NC
    slots = 8 * n_exp
    hbm = pl.BlockSpec(memory_space=pl.ANY)
    vmem = pl.BlockSpec(memory_space=pltpu.VMEM)
    mixed, grad_input, grad_gate, grad_upw, grad_down = pl.pallas_call(
        functools.partial(kernel, rows, width, hidden, head, group, n_exp),
        out_shape=(
            jax.ShapeDtypeStruct((tok_dev, width), bf16),
            jax.ShapeDtypeStruct((tok_dev, width), bf16),
            jax.ShapeDtypeStruct(gate_w.shape, bf16),
            jax.ShapeDtypeStruct(up_w.shape, bf16),
            jax.ShapeDtypeStruct(down_w.shape, bf16),
        ),
        in_specs=[hbm, hbm, hbm, vmem, vmem, vmem, hbm, hbm, hbm, hbm],
        out_specs=[vmem, vmem, hbm, hbm, hbm],
        scratch_shapes=[
            pltpu.VMEM((total, width), bf16),
            pltpu.VMEM((total, width), bf16),
            pltpu.VMEM(gate_w.shape, bf16),
            pltpu.VMEM(up_w.shape, bf16),
            pltpu.VMEM(down_w.shape, bf16),
            pltpu.VMEM((total, hidden), bf16),
            pltpu.VMEM((total, hidden), bf16),
            pltpu.VMEM((total, hidden), bf16),
            pltpu.VMEM((total, hidden), f32),
            pltpu.VMEM((total, width), bf16),
            pltpu.VMEM((total, width), bf16),
            pltpu.VMEM((2, 4, 2, rows, width), bf16),
            pltpu.VMEM((2, 2, rows, width // 2), bf16),
            pltpu.VMEM((2, 2, 2, rows, width), bf16),
            pltpu.VMEM((2, rows, width), bf16),
            pltpu.VMEM((2, rows, width), bf16),
            pltpu.VMEM(gate_w.shape, bf16),
            pltpu.VMEM(up_w.shape, bf16),
            pltpu.VMEM(down_w.shape, bf16),
            pltpu.VMEM(queries.shape, bf16),
            pltpu.VMEM((tok * NX * NY * NC, 2 * head), bf16),
            pltpu.VMEM((tok, width), bf16),
            pltpu.VMEM((tok_dev, width), bf16),
            pltpu.VMEM((3, n_exp, 8, width), bf16),
            pltpu.VMEM((3, n_exp, 8, width), bf16),
            pltpu.VMEM((n_exp, 8, tok), f32),
            pltpu.VMEM((n_exp, 8, tok), f32),
            pltpu.VMEM((tok_dev, slots), bf16),
            pltpu.VMEM((tok_dev, slots), bf16),
            pltpu.VMEM((tok_dev, slots), bf16),
            pltpu.SemaphoreType.DMA((10, 27)),
            pltpu.SemaphoreType.DMA((10, 27)),
            pltpu.SemaphoreType.DMA((12,)),
        ],
        compiler_params=pltpu.CompilerParams(
            collective_id=0, has_side_effects=True, vmem_limit_bytes=67000000
        ),
        name="layer",
    )(
        queries, keys, values, norm_gain.reshape(1, width), routes, route_scores, cotangent,
        gate_w, up_w, down_w,
    )
    return (mixed, grad_input, grad_gate[None], grad_upw[None], grad_down[None])


def solution(mesh):
    placed = (
        P("ctx", "exp"),
        P("ctx", "exp"),
        P("ctx", "exp"),
        P(),
        P(("ctx", "exp"), None),
        P(("ctx", "exp"), None),
        P(("ctx", "exp"), None),
        P("exp", None, "ctx"),
        P("exp", None, "ctx"),
        P("exp", "ctx", None),
    )
    return jax.shard_map(
        local,
        mesh=mesh,
        in_specs=placed,
        out_specs=(
            P(("ctx", "exp"), None),
            P(("ctx", "exp"), None),
            P("exp", None, "ctx"),
            P("exp", None, "ctx"),
            P("exp", "ctx", None),
        ),
        check_vma=False,
    )
```

```python
import functools

import jax
import jax.numpy as jnp
from jax import lax
from jax.experimental import pallas as pl
from jax.experimental.pallas import tpu as pltpu
from jax.sharding import PartitionSpec as P

norm_eps = 1e-05
masked_value = -1e30
NX, NY, NC = 4, 2, 2
f32, bf16 = jnp.float32, jnp.bfloat16


class Place:
    def __init__(self):
        c = lax.axis_index("ctx")
        self.k = lax.rem(c, NC)
        self.x = lax.rem(lax.div(c, NC), NX)
        self.y = lax.div(c, NC * NX)
        self.ok = 1 - self.k
        self.oy = 1 - self.y
        self.xr = lax.rem(self.x + 1, NX)
        self.xl = lax.rem(self.x + 3, NX)
        self.xf = lax.rem(self.x + 2, NX)
        self.partner = self.index(self.x, self.y, self.ok)
        self.across = self.index(self.x, self.oy, self.k)
        self.right = self.index(self.xr, self.y, self.k)
        self.left = self.index(self.xl, self.y, self.k)

    def index(self, x, y, k):
        return (y * NX + x) * NC + k


class Copies:
    def __init__(self, send, recv, tensor, axis="ctx"):
        self.send, self.recv, self.tensor, self.axis = send, recv, tensor, axis
        self.started, self.count = [], 0

    def start(self, src, dst, device, arrival):
        copy = pltpu.make_async_remote_copy(
            src_ref=src, dst_ref=dst,
            send_sem=self.send.at[self.tensor, self.count],
            recv_sem=self.recv.at[self.tensor, arrival],
            device_id={self.axis: device}, device_id_type=pl.DeviceIdType.MESH,
        )
        copy.start()
        self.started.append(copy)
        self.count += 1

    def arrived(self, ref, arrival, device):
        pltpu.make_async_remote_copy(
            src_ref=ref, dst_ref=ref,
            send_sem=self.send.at[self.tensor, 0],
            recv_sem=self.recv.at[self.tensor, arrival],
            device_id={self.axis: device}, device_id_type=pl.DeviceIdType.MESH,
        ).wait_recv()

    def drain(self):
        for copy in self.started:
            copy.wait_send()


class Gather:
    def __init__(self, copies, buf, rows, width, place, over_y=False):
        self.c, self.buf, self.rows, self.width, self.p = copies, buf, rows, width, place
        self.over_y = over_y

    def block(self, x, y, k, half=None):
        start = pl.multiple_of(((x * NY + y) * NC + k) * self.rows, 16)
        if half is None:
            return self.buf.at[pl.ds(start, self.rows), :]
        mid = self.width // 2
        return self.buf.at[pl.ds(start, self.rows), pl.ds(half * mid, mid)]

    def send(self, ref, device, arrival):
        self.c.start(ref, ref, device, arrival)

    def own(self):
        p = self.p
        mine = self.block(p.x, p.y, p.k)
        self.send(mine, p.across, 0)
        self.send(mine, p.right, 1)
        self.send(mine, p.left, 2)
        self.send(mine, p.partner, 9)

    def across(self):
        p = self.p
        got = self.block(p.x, p.oy, p.k)
        self.c.arrived(got, 0, p.across)
        self.send(got, p.right, 3)
        self.send(got, p.left, 4)
        self.send(got, p.partner, 10)

    def beside(self, stage):
        p = self.p
        y = p.oy if stage else p.y
        got = self.block(p.xl, y, p.k)
        self.c.arrived(got, 1 + 2 * stage, p.left)
        if not (stage and self.over_y):
            self.send(self.block(p.xl, y, p.k, 0), p.right, 5 + 2 * stage)
        self.send(got, p.partner, 11 + 2 * stage)
        got = self.block(p.xr, y, p.k)
        self.c.arrived(got, 2 + 2 * stage, p.right)
        if not (stage and self.over_y):
            self.send(self.block(p.xr, y, p.k, 1), p.left, 6 + 2 * stage)
        self.send(got, p.partner, 12 + 2 * stage)

    def far(self, stage):
        p = self.p
        y = p.oy if stage else p.y
        if stage and self.over_y:
            self.c.arrived(self.block(p.xf, y, p.k), 7, p.across)
        else:
            self.c.arrived(self.block(p.xf, y, p.k, 0), 5 + 2 * stage, p.left)
            self.c.arrived(self.block(p.xf, y, p.k, 1), 6 + 2 * stage, p.right)
        if self.over_y and not stage:
            self.send(self.block(p.xf, y, p.k), p.across, 7)
        self.send(self.block(p.xf, y, p.k), p.partner, 15 + stage)

    def other_core(self, which):
        p = self.p
        spots = {
            "own": [(p.x, p.y, 9), (p.x, p.oy, 10)],
            "left": [(p.xl, p.y, 11), (p.xl, p.oy, 13)],
            "right": [(p.xr, p.y, 12), (p.xr, p.oy, 14)],
            "far": [(p.xf, p.y, 15), (p.xf, p.oy, 16)],
        }[which]
        for x, y, arrival in spots:
            self.c.arrived(self.block(x, y, p.ok), arrival, p.partner)

    def all_but_own(self):
        self.across()
        for stage in range(2):
            self.beside(stage)
        for stage in range(2):
            self.far(stage)
        for which in ("own", "left", "right", "far"):
            self.other_core(which)


def add_into(dst, rows, count, width, first, sources):
    step = 768

    @pl.loop(0, width // step)
    def _(i):
        at = pl.multiple_of(i * step, 128)
        spot = pl.multiple_of(first + i * step, 128)
        total = dst[pl.ds(rows, count), pl.ds(spot, step)].astype(f32)
        for source in sources:
            total = total + source[:, pl.ds(at, step)].astype(f32)
        dst[pl.ds(rows, count), pl.ds(spot, step)] = total.astype(bf16)


class Reduce:
    def __init__(
        self, copies, buf, core_in, far_in, near_in, across_in, far_across_in, rows, width, place
    ):
        self.c, self.buf, self.p, self.rows, self.width = copies, buf, place, rows, width
        self.core_in, self.far_in, self.near_in, self.across_in = core_in, far_in, near_in, across_in
        self.far_across_in = far_across_in

    def start_of(self, x, y, k):
        return pl.multiple_of(((x * NY + y) * NC + k) * self.rows, 16)

    def block(self, x, y, k):
        return self.buf.at[pl.ds(self.start_of(x, y, k), self.rows), :]

    def half(self, x, y, k, half):
        mid = self.width // 2
        return self.buf.at[pl.ds(self.start_of(x, y, k), self.rows), pl.ds(half * mid, mid)]

    def columns(self):
        p = self.p
        return [p.x, p.xr, p.xl, p.xf]

    def core_send(self, which):
        p = self.p
        x = self.columns()[which]
        for j, y in enumerate((p.oy, p.y)):
            self.c.start(
                self.block(x, y, p.ok), self.core_in.at[which, j], p.partner, which * 2 + j
            )

    def core_add(self, which):
        p = self.p
        x = self.columns()[which]
        for j, y in enumerate((p.oy, p.y)):
            self.c.arrived(self.core_in.at[which, j], which * 2 + j, p.partner)
            add_into(
                self.buf, self.start_of(x, y, p.k), self.rows, self.width, 0,
                [self.core_in.at[which, j]],
            )

    def near_early(self, side):
        p = self.p
        x, device = ((p.xr, p.right), (p.xl, p.left))[side]
        self.c.start(self.block(x, p.oy, p.k), self.near_in.at[side, 0], device, 12 + 2 * side)

    def far_across(self):
        p = self.p
        self.c.start(self.block(p.xf, p.oy, p.k), self.far_across_in, p.across, 17)

    def far_send(self):
        p = self.p
        self.c.arrived(self.far_across_in, 17, p.across)
        add_into(
            self.buf, self.start_of(p.xf, p.y, p.k), self.rows, self.width, 0, [self.far_across_in]
        )
        self.c.start(self.half(p.xf, p.y, p.k, 0), self.far_in.at[0], p.right, 8)
        self.c.start(self.half(p.xf, p.y, p.k, 1), self.far_in.at[1], p.left, 9)

    def near_send(self):
        p = self.p
        mid = self.width // 2
        self.c.arrived(self.far_in.at[0], 8, p.left)
        add_into(self.buf, self.start_of(p.xr, p.y, p.k), self.rows, mid, 0, [self.far_in.at[0]])
        self.c.start(self.block(p.xr, p.y, p.k), self.near_in.at[0, 1], p.right, 13)
        self.c.arrived(self.far_in.at[1], 9, p.right)
        add_into(self.buf, self.start_of(p.xl, p.y, p.k), self.rows, mid, mid, [self.far_in.at[1]])
        self.c.start(self.block(p.xl, p.y, p.k), self.near_in.at[1, 1], p.left, 15)

    def near_add(self, j):
        p = self.p
        y = (p.oy, p.y)[j]
        self.c.arrived(self.near_in.at[0, j], 12 + j, p.left)
        self.c.arrived(self.near_in.at[1, j], 14 + j, p.right)
        add_into(
            self.buf, self.start_of(p.x, y, p.k), self.rows, self.width, 0,
            [self.near_in.at[0, j], self.near_in.at[1, j]],
        )
        if j == 0:
            self.c.start(self.block(p.x, y, p.k), self.across_in, p.across, 16)

    def finish(self):
        p = self.p
        self.c.arrived(self.across_in, 16, p.across)
        add_into(
            self.buf, self.start_of(p.x, p.y, p.k), self.rows, self.width, 0, [self.across_in]
        )


def dot(a, b, dims=((1,), (0,))):
    return lax.dot_general(a, b, (dims, ((), ())), preferred_element_type=f32)


class HeadGather:
    def __init__(self, copies, buf, head, group, e):
        self.c, self.buf, self.head, self.group = copies, buf, head, group
        hi, z = lax.div(e, 4), lax.rem(e, 4)
        up, down, far = [lax.rem(z + d, 4) for d in (1, 3, 2)]
        self.e = e
        self.mirror = (1 - hi) * 4 + z
        self.up, self.down = hi * 4 + up, hi * 4 + down
        self.ups = [self.up, (1 - hi) * 4 + up]
        self.downs = [self.down, (1 - hi) * 4 + down]
        self.fars = [hi * 4 + far, (1 - hi) * 4 + far]

    def block(self, e, h, half=None):
        spot = pl.multiple_of((e * self.group + h) * self.head, 128)
        if half is None:
            return self.buf.at[:, pl.ds(spot, self.head)]
        count = self.buf.shape[0] // 2
        return self.buf.at[pl.ds(half * count, count), pl.ds(spot, self.head)]

    def own(self, h):
        mine = self.block(self.e, h)
        self.c.start(mine, mine, self.mirror, h * 9)
        self.c.start(mine, mine, self.up, h * 9 + 1)
        self.c.start(mine, mine, self.down, h * 9 + 2)

    def relay(self, h):
        got = self.block(self.mirror, h)
        self.c.arrived(got, h * 9, self.mirror)
        self.c.start(got, got, self.up, h * 9 + 3)
        self.c.start(got, got, self.down, h * 9 + 4)

    def forward(self, h):
        for i in range(2):
            self.c.arrived(self.block(self.downs[i], h), h * 9 + 1 + 2 * i, self.down)
            part = self.block(self.downs[i], h, 0)
            self.c.start(part, part, self.up, h * 9 + 5 + 2 * i)
            self.c.arrived(self.block(self.ups[i], h), h * 9 + 2 + 2 * i, self.up)
            part = self.block(self.ups[i], h, 1)
            self.c.start(part, part, self.down, h * 9 + 6 + 2 * i)

    def rest(self, h):
        for i in range(2):
            self.c.arrived(self.block(self.fars[i], h, 0), h * 9 + 5 + 2 * i, self.down)
            self.c.arrived(self.block(self.fars[i], h, 1), h * 9 + 6 + 2 * i, self.up)


class Exchange:
    def __init__(self, copies, out, into, sem, e, n):
        self.c, self.out, self.into, self.e, self.n = copies, out, into, e, n
        self.kept = pltpu.make_async_copy(out.at[e], into.at[e], sem)

    def start(self):
        for d in range(1, self.n):
            peer = lax.rem(self.e + d, self.n)
            self.c.start(self.out.at[peer], self.into.at[self.e], peer, d - 1)
        self.kept.start()

    def finish(self):
        self.kept.wait()
        for d in range(1, self.n):
            peer = lax.rem(self.e + self.n - d, self.n)
            self.c.arrived(self.into.at[peer], d - 1, peer)


def dot(a, b, dims=((1,), (0,))):
    return lax.dot_general(a, b, (dims, ((), ())), preferred_element_type=f32)


def iota(shape, axis):
    return lax.broadcasted_iota(jnp.int32, shape, axis)


def kernel(
    rows, width, hidden, head, group, n_exp,
    q_hbm, k_hbm, v_hbm, gain, routes, scores, cot_hbm, wg_hbm, wu_hbm, wd_hbm,
    mixed_out, gi_out, gg, gu, gd,
    xbuf, dybuf, wg, wu, wd, hid, dgb, dub, dhb, py, px,
    core_in, far_in, near_in, across_in, far_across_in,
    q, kv, attn, cot, slabs_out, slabs_in, spots_out, spots_in, place, mix_hi, mix_lo,
    send, recv, local_sem,
):
    p = Place()
    e = lax.axis_index("exp")
    mesh_id = pl.DeviceIdType.MESH
    tok = q.shape[0]
    tok_dev = cot.shape[0]
    slot = 8
    slots = n_exp * slot
    barrier = pltpu.get_barrier_semaphore()
    for device in (p.partner, p.across, p.right, p.left):
        pl.semaphore_signal(barrier, inc=1, device_id={"ctx": device}, device_id_type=mesh_id)
    for d in range(1, n_exp):
        pl.semaphore_signal(
            barrier, inc=1, device_id={"exp": lax.rem(e + d, n_exp)}, device_id_type=mesh_id
        )

    def copies(tensor, axis="ctx"):
        return Copies(send, recv, tensor, axis)

    gx = Gather(copies(0), xbuf, rows, width, p, True)
    gy = Gather(copies(1), dybuf, rows, width, p, True)
    ry = Reduce(copies(2), py, core_in.at[0], far_in.at[0], near_in.at[0],
                across_in.at[0], far_across_in.at[0], rows, width, p)
    rx = Reduce(copies(3), px, core_in.at[1], far_in.at[1], near_in.at[1],
                across_in.at[1], far_across_in.at[1], rows, width, p)
    gk = Gather(copies(4), kv, tok, 2 * head, p)
    ga = HeadGather(copies(5, "exp"), attn, head, group, e)
    grads_there = Exchange(copies(6, "exp"), slabs_out.at[0], slabs_in.at[0], local_sem.at[8], e, n_exp)
    spots_there = Exchange(copies(7, "exp"), spots_out, spots_in, local_sem.at[9], e, n_exp)
    y_back = Exchange(copies(8, "exp"), slabs_out.at[1], slabs_in.at[1], local_sem.at[10], e, n_exp)
    dx_back = Exchange(copies(9, "exp"), slabs_out.at[2], slabs_in.at[2], local_sem.at[11], e, n_exp)

    own = pl.ds(pl.multiple_of(((p.x * NY + p.y) * NC + p.k) * tok, 16), tok)
    first = [
        pltpu.make_async_copy(k_hbm, kv.at[own, pl.ds(0, head)], local_sem.at[0]),
        pltpu.make_async_copy(v_hbm, kv.at[own, pl.ds(head, head)], local_sem.at[1]),
        pltpu.make_async_copy(cot_hbm, cot, local_sem.at[2]),
        pltpu.make_async_copy(q_hbm, q, local_sem.at[3]),
    ]
    loads = [
        pltpu.make_async_copy(src, dst, local_sem.at[4 + i])
        for i, (src, dst) in enumerate(((wd_hbm, wd), (wg_hbm, wg), (wu_hbm, wu)))
    ]
    for copy in first + loads:
        copy.start()

    lane = iota((tok_dev, slots), 1)
    expert, order = lane >> 3, lane & 7
    in_a = routes[:, 0:1] == expert
    in_b = routes[:, 1:2] == expert
    named = jnp.where(in_a | in_b, 1.0, 0.0)
    earlier = jnp.where(iota((tok_dev, tok_dev), 1) < iota((tok_dev, tok_dev), 0), 1.0, 0.0)
    rank = dot(earlier.astype(bf16), named.astype(bf16))
    here = (named > 0.5) & (rank.astype(jnp.int32) == order)
    top = jnp.max(scores[...], axis=1, keepdims=True)
    odds_a, odds_b = jnp.exp(scores[:, 0:1] - top), jnp.exp(scores[:, 1:2] - top)
    whole = odds_a + odds_b
    mix = jnp.where(here, jnp.where(in_a, odds_a / whole, odds_b / whole), 0.0)
    placed = jnp.where(here, 1.0, 0.0).astype(bf16)
    upper = mix.astype(bf16)
    lower = (mix - upper.astype(f32)).astype(bf16)
    place[...] = placed
    mix_hi[...] = upper
    mix_lo[...] = lower
    shift = jnp.where(
        iota((tok_dev, tok), 1) == iota((tok_dev, tok), 0) + e * tok_dev, 1.0, 0.0
    ).astype(bf16)
    spots_out[...] = dot(placed, shift, ((0,), (0,))).reshape(n_exp, slot, tok)

    pl.semaphore_wait(barrier, 3 + n_exp)
    first[0].wait()
    first[1].wait()
    gk.own()
    spots_there.start()
    first[2].wait()
    chunk = 512

    @pl.loop(0, width // chunk)
    def _(n):
        spot = pl.ds(pl.multiple_of(n * chunk, 128), chunk)
        part = dot(mix_hi[...], cot[:, spot], ((0,), (0,))) + dot(mix_lo[...], cot[:, spot], ((0,), (0,)))
        slabs_out[0, :, :, spot] = part.reshape(n_exp, slot, chunk).astype(bf16)

    grads_there.start()
    row, from_row = iota((rows, slots), 0), iota((rows, slots), 1)
    source = (row * 43) >> 8
    squeeze = jnp.where(from_row == source * slot + (row - source * 6), 1.0, 0.0).astype(bf16)
    gk.across()
    gk.beside(0)
    gk.beside(1)
    gk.far(0)
    gk.far(1)
    spots_there.finish()
    pick = dot(squeeze, spots_in[...].reshape(slots, tok).astype(bf16)).astype(bf16)
    grads_there.finish()
    own_rows = pl.ds(pl.multiple_of(((p.x * NY + p.y) * NC + p.k) * rows, 16), rows)

    @pl.loop(0, width // chunk)
    def _(n):
        spot = pl.ds(pl.multiple_of(n * chunk, 128), chunk)
        slabs = slabs_in[0, :, :, spot].astype(f32).reshape(slots, chunk).astype(bf16)
        dybuf[own_rows, spot] = dot(squeeze, slabs).astype(bf16)

    gy.own()
    first[3].wait()
    for which in ("own", "left", "right", "far"):
        gk.other_core(which)
    total_keys = kv.shape[0]
    at = iota((1, total_keys), 1)
    block = at // tok
    key_pos = (((block >> 1) & 1) * NX * NC + (block >> 2) * NC + (block & 1)) * tok + at % tok
    query_pos = lax.axis_index("ctx") * tok + iota((tok, 1), 0)
    for h in range(group):
        s = dot(q[:, h * head : (h + 1) * head], kv[:, 0:head], ((1,), (1,))) * head ** (-0.5)
        s = jnp.where(key_pos <= query_pos, s, masked_value)
        weights = jnp.exp(s - jnp.max(s, axis=1, keepdims=True))
        total = jnp.sum(weights, axis=1, keepdims=True)
        out = dot(weights.astype(bf16), kv[:, head : 2 * head]) / total
        spot = pl.multiple_of((e * group + h) * head, 128)
        attn[:, pl.ds(spot, head)] = out.astype(bf16)
        ga.own(h)
    for h in range(group):
        ga.relay(h)
    gy.beside(0)
    gy.across()
    for h in range(group):
        ga.forward(h)
    for h in range(group):
        ga.rest(h)
    gy.far(0)

    def squares(n, total):
        part = attn[:, pl.ds(pl.multiple_of(n * chunk, 128), chunk)].astype(f32)
        return total + jnp.sum(part * part, axis=1, keepdims=True)

    total = lax.fori_loop(0, width // chunk, squares, jnp.zeros((tok, 1), f32))
    inv = lax.rsqrt(total / width + norm_eps)

    @pl.loop(0, width // chunk)
    def _(n):
        spot = pl.ds(pl.multiple_of(n * chunk, 128), chunk)
        normed = (attn[:, spot].astype(f32) * inv * gain[:, spot]).astype(bf16)
        xbuf[own_rows, spot] = dot(pick, normed).astype(bf16)

    gx.own()
    for copy in loads:
        copy.wait()
    col = NY * NC * rows
    tile = 256
    wtile = 512

    def back_half(x):
        at = pl.multiple_of(x * col, 16)

        @pl.loop(0, hidden // tile)
        def _(n):
            spot = pl.ds(pl.multiple_of(n * tile, 128), tile)
            dhb[pl.ds(at, col), spot] = dot(dybuf[pl.ds(at, col), :], wd[spot, :], ((1,), (1,)))

    def first_half(x):
        at = pl.multiple_of(x * col, 16)

        @pl.loop(0, hidden // tile)
        def _(n):
            cols = pl.ds(pl.multiple_of(n * tile, 128), tile)
            xs = xbuf[pl.ds(at, col), :]
            g = dot(xs, wg[:, cols])
            u = dot(xs, wu[:, cols])
            dh = dhb[pl.ds(at, col), cols]
            sig = 1.0 / (1.0 + jnp.exp(-g))
            silu = g * sig
            hid[pl.ds(at, col), cols] = (silu * u).astype(bf16)
            dub[pl.ds(at, col), cols] = (dh * silu).astype(bf16)
            dgb[pl.ds(at, col), cols] = (dh * u * sig * (1.0 + g * (1.0 - sig))).astype(bf16)

    def expert_out(x):
        at = pl.multiple_of(x * col, 16)

        @pl.loop(0, width // wtile)
        def _(n):
            spot = pl.ds(pl.multiple_of(n * wtile, 128), wtile)
            py[pl.ds(at, col), spot] = dot(hid[pl.ds(at, col), :], wd[:, spot]).astype(bf16)

    def input_grad(x):
        at = pl.multiple_of(x * col, 16)

        @pl.loop(0, width // wtile)
        def _(n):
            spot = pl.ds(pl.multiple_of(n * wtile, 128), wtile)
            px[pl.ds(at, col), spot] = (
                dot(dgb[pl.ds(at, col), :], wg[spot, :], ((1,), (1,)))
                + dot(dub[pl.ds(at, col), :], wu[spot, :], ((1,), (1,)))
            ).astype(bf16)

    def weight_grads(begin, end):
        @pl.loop(begin, end)
        def _(n):
            spot = pl.ds(pl.multiple_of(n * wtile, 128), wtile)
            gd[:, spot] = dot(hid[...], dybuf[:, spot], ((0,), (0,))).astype(bf16)
            xt = xbuf[:, spot]
            gg[spot, :] = dot(xt, dgb[...], ((0,), (0,))).astype(bf16)
            gu[spot, :] = dot(xt, dub[...], ((0,), (0,))).astype(bf16)

    def rest_of_column(which, x):
        expert_out(x)
        ry.core_send(which)
        input_grad(x)
        rx.core_send(which)

    def near_early(which):
        for work in (ry, rx):
            work.core_add(which)
            work.near_early(which - 1)

    def to_slabs(buf, which):
        row, to_row = iota((slots, rows), 1), iota((slots, rows), 0)
        source = (row * 43) >> 8
        spread = jnp.where(to_row == source * slot + (row - source * 6), 1.0, 0.0).astype(bf16)

        @pl.loop(0, width // chunk)
        def _(n):
            spot = pl.ds(pl.multiple_of(n * chunk, 128), chunk)
            part = dot(spread, buf[own_rows, spot])
            slabs_out[which, :, :, spot] = part.reshape(n_exp, slot, chunk).astype(bf16)

    def from_slabs(which, spot):
        return slabs_in[which, :, :, spot].astype(f32).reshape(slots, chunk).astype(bf16)

    gy.beside(1)
    gy.other_core("own")
    back_half(p.x)
    gy.other_core("right")
    gy.other_core("left")
    back_half(p.xr)
    back_half(p.xl)
    gy.far(1)
    gx.beside(0)
    gx.across()
    gx.other_core("own")
    first_half(p.x)
    rest_of_column(0, p.x)
    gx.far(0)
    gy.other_core("far")
    back_half(p.xf)
    gx.beside(1)
    gx.other_core("right")
    first_half(p.xr)
    rest_of_column(1, p.xr)
    gx.other_core("left")
    first_half(p.xl)
    near_early(1)
    rest_of_column(2, p.xl)
    gx.far(1)
    gx.other_core("far")
    first_half(p.xf)
    near_early(2)
    rest_of_column(3, p.xf)
    ry.core_add(3)
    ry.far_across()
    rx.core_add(3)
    rx.far_across()
    ry.core_add(0)
    rx.core_add(0)
    weight_grads(0, 2)
    ry.far_send()
    ry.near_add(0)
    weight_grads(2, 3)
    rx.far_send()
    rx.near_add(0)
    weight_grads(3, 4)
    ry.near_send()
    weight_grads(4, 5)
    rx.near_send()
    weight_grads(5, width // wtile)
    ry.near_add(1)
    ry.finish()
    to_slabs(py, 1)
    y_back.start()
    rx.near_add(1)
    rx.finish()
    to_slabs(px, 2)
    dx_back.start()
    y_back.finish()

    @pl.loop(0, width // chunk)
    def _(n):
        spot = pl.ds(pl.multiple_of(n * chunk, 128), chunk)
        slabs = from_slabs(1, spot)
        mixed_out[:, spot] = (dot(mix_hi[...], slabs) + dot(mix_lo[...], slabs)).astype(bf16)

    dx_back.finish()
    mine = pl.ds(pl.multiple_of(e * tok_dev, 16), tok_dev)
    feats = attn[mine, :].astype(f32)
    inv_own = lax.rsqrt(jnp.sum(feats * feats, axis=1, keepdims=True) / width + norm_eps)
    back = slabs_in[2].astype(f32).reshape(slots, width).astype(bf16)
    weighted = dot(place[...], back) * gain[...]
    inner = jnp.sum(weighted * feats, axis=1, keepdims=True) / width
    gi_out[...] = (inv_own * weighted - feats * (inv_own * inv_own * inv_own * inner)).astype(bf16)
    for work in (gx, gy, ry, rx, gk, ga, grads_there, spots_there, y_back, dx_back):
        work.c.drain()


def put_out(*refs):
    n = len(refs) // 2
    copies = [
        pltpu.make_async_copy(refs[i], refs[n + i], refs[-1].at[i]) for i in range(n)
    ]
    for copy in copies:
        copy.start()
    for copy in copies:
        copy.wait()


def local(queries, keys, values, norm_gain, routes, route_scores, cotangent, w_gate, w_up, w_down):
    n_exp = lax.axis_size("exp")
    head = keys.shape[1]
    group = queries.shape[1] // head
    tok = queries.shape[0]
    tok_dev, width = cotangent.shape
    rows = 3 * tok_dev
    gate_w, up_w, down_w = w_gate[0], w_up[0], w_down[0]
    hidden = gate_w.shape[1]
    total = rows * NX * NY * NC
    slots = 8 * n_exp
    hbm = pl.BlockSpec(memory_space=pl.ANY)
    vmem = pl.BlockSpec(memory_space=pltpu.VMEM)
    mixed, grad_input, grad_gate, grad_upw, grad_down = pl.pallas_call(
        functools.partial(kernel, rows, width, hidden, head, group, n_exp),
        out_shape=(
            pltpu.VMEM((tok_dev, width), bf16),
            pltpu.VMEM((tok_dev, width), bf16),
            pltpu.VMEM(gate_w.shape, bf16),
            pltpu.VMEM(up_w.shape, bf16),
            pltpu.VMEM(down_w.shape, bf16),
        ),
        in_specs=[hbm, hbm, hbm, vmem, vmem, vmem, hbm, hbm, hbm, hbm],
        out_specs=[vmem] * 5,
        scratch_shapes=[
            pltpu.VMEM((total, width), bf16),
            pltpu.VMEM((total, width), bf16),
            pltpu.VMEM(gate_w.shape, bf16),
            pltpu.VMEM(up_w.shape, bf16),
            pltpu.VMEM(down_w.shape, bf16),
            pltpu.VMEM((total, hidden), bf16),
            pltpu.VMEM((total, hidden), bf16),
            pltpu.VMEM((total, hidden), bf16),
            pltpu.VMEM((total, hidden), f32),
            pltpu.VMEM((total, width), bf16),
            pltpu.VMEM((total, width), bf16),
            pltpu.VMEM((2, 4, 2, rows, width), bf16),
            pltpu.VMEM((2, 2, rows, width // 2), bf16),
            pltpu.VMEM((2, 2, 2, rows, width), bf16),
            pltpu.VMEM((2, rows, width), bf16),
            pltpu.VMEM((2, rows, width), bf16),
            pltpu.VMEM(queries.shape, bf16),
            pltpu.VMEM((tok * NX * NY * NC, 2 * head), bf16),
            pltpu.VMEM((tok, width), bf16),
            pltpu.VMEM((tok_dev, width), bf16),
            pltpu.VMEM((3, n_exp, 8, width), bf16),
            pltpu.VMEM((3, n_exp, 8, width), bf16),
            pltpu.VMEM((n_exp, 8, tok), f32),
            pltpu.VMEM((n_exp, 8, tok), f32),
            pltpu.VMEM((tok_dev, slots), bf16),
            pltpu.VMEM((tok_dev, slots), bf16),
            pltpu.VMEM((tok_dev, slots), bf16),
            pltpu.SemaphoreType.DMA((10, 27)),
            pltpu.SemaphoreType.DMA((10, 27)),
            pltpu.SemaphoreType.DMA((12,)),
        ],
        compiler_params=pltpu.CompilerParams(
            collective_id=0, has_side_effects=True, vmem_limit_bytes=54000000
        ),
        name="layer",
    )(
        queries, keys, values, norm_gain.reshape(1, width), routes, route_scores, cotangent,
        gate_w, up_w, down_w,
    )
    results = (mixed, grad_input, grad_gate, grad_upw, grad_down)
    mixed, grad_input, grad_gate, grad_upw, grad_down = pl.pallas_call(
        put_out,
        out_shape=tuple(jax.ShapeDtypeStruct(r.shape, r.dtype) for r in results),
        in_specs=[hbm] * 5,
        out_specs=[hbm] * 5,
        scratch_shapes=[pltpu.SemaphoreType.DMA((5,))],
        compiler_params=pltpu.CompilerParams(vmem_limit_bytes=1000000),
        name="put_out",
    )(*results)
    return (mixed, grad_input, grad_gate[None], grad_upw[None], grad_down[None])


def solution(mesh):
    placed = (
        P("ctx", "exp"),
        P("ctx", "exp"),
        P("ctx", "exp"),
        P(),
        P(("ctx", "exp"), None),
        P(("ctx", "exp"), None),
        P(("ctx", "exp"), None),
        P("exp", None, "ctx"),
        P("exp", None, "ctx"),
        P("exp", "ctx", None),
    )
    return jax.shard_map(
        local,
        mesh=mesh,
        in_specs=placed,
        out_specs=(
            P(("ctx", "exp"), None),
            P(("ctx", "exp"), None),
            P("exp", None, "ctx"),
            P("exp", None, "ctx"),
            P("exp", "ctx", None),
        ),
        check_vma=False,
    )
```

```python
import functools

import jax
import jax.numpy as jnp
from jax import lax
from jax.experimental import pallas as pl
from jax.experimental.pallas import tpu as pltpu
from jax.sharding import PartitionSpec as P

norm_eps = 1e-05
masked_value = -1e30
NX, NY, NC = 4, 2, 2
f32, bf16 = jnp.float32, jnp.bfloat16


class Place:
    def __init__(self):
        c = lax.axis_index("ctx")
        self.k = lax.rem(c, NC)
        self.x = lax.rem(lax.div(c, NC), NX)
        self.y = lax.div(c, NC * NX)
        self.ok = 1 - self.k
        self.oy = 1 - self.y
        self.xr = lax.rem(self.x + 1, NX)
        self.xl = lax.rem(self.x + 3, NX)
        self.xf = lax.rem(self.x + 2, NX)
        self.partner = self.index(self.x, self.y, self.ok)
        self.across = self.index(self.x, self.oy, self.k)
        self.right = self.index(self.xr, self.y, self.k)
        self.left = self.index(self.xl, self.y, self.k)

    def index(self, x, y, k):
        return (y * NX + x) * NC + k


class Copies:
    def __init__(self, send, recv, tensor, axis="ctx"):
        self.send, self.recv, self.tensor, self.axis = send, recv, tensor, axis
        self.started, self.count = [], 0

    def start(self, src, dst, device, arrival):
        copy = pltpu.make_async_remote_copy(
            src_ref=src, dst_ref=dst,
            send_sem=self.send.at[self.tensor, self.count],
            recv_sem=self.recv.at[self.tensor, arrival],
            device_id={self.axis: device}, device_id_type=pl.DeviceIdType.MESH,
        )
        copy.start()
        self.started.append(copy)
        self.count += 1

    def arrived(self, ref, arrival, device):
        pltpu.make_async_remote_copy(
            src_ref=ref, dst_ref=ref,
            send_sem=self.send.at[self.tensor, 0],
            recv_sem=self.recv.at[self.tensor, arrival],
            device_id={self.axis: device}, device_id_type=pl.DeviceIdType.MESH,
        ).wait_recv()

    def drain(self):
        for copy in self.started:
            copy.wait_send()


class Gather:
    def __init__(self, copies, buf, rows, width, place, over_y=False):
        self.c, self.buf, self.rows, self.width, self.p = copies, buf, rows, width, place
        self.over_y = over_y

    def block(self, x, y, k, half=None):
        start = pl.multiple_of(((x * NY + y) * NC + k) * self.rows, 16)
        if half is None:
            return self.buf.at[pl.ds(start, self.rows), :]
        mid = self.width // 2
        return self.buf.at[pl.ds(start, self.rows), pl.ds(half * mid, mid)]

    def send(self, ref, device, arrival):
        self.c.start(ref, ref, device, arrival)

    def own(self):
        p = self.p
        mine = self.block(p.x, p.y, p.k)
        self.send(mine, p.across, 0)
        self.send(mine, p.right, 1)
        self.send(mine, p.left, 2)
        self.send(mine, p.partner, 9)

    def across(self):
        p = self.p
        got = self.block(p.x, p.oy, p.k)
        self.c.arrived(got, 0, p.across)
        self.send(got, p.right, 3)
        self.send(got, p.left, 4)
        self.send(got, p.partner, 10)

    def beside(self, stage):
        p = self.p
        y = p.oy if stage else p.y
        got = self.block(p.xl, y, p.k)
        self.c.arrived(got, 1 + 2 * stage, p.left)
        if not (stage and self.over_y):
            self.send(self.block(p.xl, y, p.k, 0), p.right, 5 + 2 * stage)
        self.send(got, p.partner, 11 + 2 * stage)
        got = self.block(p.xr, y, p.k)
        self.c.arrived(got, 2 + 2 * stage, p.right)
        if not (stage and self.over_y):
            self.send(self.block(p.xr, y, p.k, 1), p.left, 6 + 2 * stage)
        self.send(got, p.partner, 12 + 2 * stage)

    def far(self, stage):
        p = self.p
        y = p.oy if stage else p.y
        if stage and self.over_y:
            self.c.arrived(self.block(p.xf, y, p.k), 7, p.across)
        else:
            self.c.arrived(self.block(p.xf, y, p.k, 0), 5 + 2 * stage, p.left)
            self.c.arrived(self.block(p.xf, y, p.k, 1), 6 + 2 * stage, p.right)
        if self.over_y and not stage:
            self.send(self.block(p.xf, y, p.k), p.across, 7)
        self.send(self.block(p.xf, y, p.k), p.partner, 15 + stage)

    def other_core(self, which):
        p = self.p
        spots = {
            "own": [(p.x, p.y, 9), (p.x, p.oy, 10)],
            "left": [(p.xl, p.y, 11), (p.xl, p.oy, 13)],
            "right": [(p.xr, p.y, 12), (p.xr, p.oy, 14)],
            "far": [(p.xf, p.y, 15), (p.xf, p.oy, 16)],
        }[which]
        for x, y, arrival in spots:
            self.c.arrived(self.block(x, y, p.ok), arrival, p.partner)

    def all_but_own(self):
        self.across()
        for stage in range(2):
            self.beside(stage)
        for stage in range(2):
            self.far(stage)
        for which in ("own", "left", "right", "far"):
            self.other_core(which)


def add_into(dst, rows, count, width, first, sources):
    step = 768

    @pl.loop(0, width // step, unroll=True)
    def _(i):
        at = pl.multiple_of(i * step, 128)
        spot = pl.multiple_of(first + i * step, 128)
        total = dst[pl.ds(rows, count), pl.ds(spot, step)].astype(f32)
        for source in sources:
            total = total + source[:, pl.ds(at, step)].astype(f32)
        dst[pl.ds(rows, count), pl.ds(spot, step)] = total.astype(bf16)


class Reduce:
    def __init__(
        self, copies, buf, core_in, far_in, near_in, across_in, far_across_in, rows, width, place
    ):
        self.c, self.buf, self.p, self.rows, self.width = copies, buf, place, rows, width
        self.core_in, self.far_in, self.near_in, self.across_in = core_in, far_in, near_in, across_in
        self.far_across_in = far_across_in

    def start_of(self, x, y, k):
        return pl.multiple_of(((x * NY + y) * NC + k) * self.rows, 16)

    def block(self, x, y, k):
        return self.buf.at[pl.ds(self.start_of(x, y, k), self.rows), :]

    def half(self, x, y, k, half):
        mid = self.width // 2
        return self.buf.at[pl.ds(self.start_of(x, y, k), self.rows), pl.ds(half * mid, mid)]

    def columns(self):
        p = self.p
        return [p.x, p.xr, p.xl, p.xf]

    def core_send(self, which):
        p = self.p
        x = self.columns()[which]
        for j, y in enumerate((p.oy, p.y)):
            self.c.start(
                self.block(x, y, p.ok), self.core_in.at[which, j], p.partner, which * 2 + j
            )

    def core_add(self, which):
        p = self.p
        x = self.columns()[which]
        for j, y in enumerate((p.oy, p.y)):
            self.c.arrived(self.core_in.at[which, j], which * 2 + j, p.partner)
            add_into(
                self.buf, self.start_of(x, y, p.k), self.rows, self.width, 0,
                [self.core_in.at[which, j]],
            )

    def near_early(self, side):
        p = self.p
        x, device = ((p.xr, p.right), (p.xl, p.left))[side]
        self.c.start(self.block(x, p.oy, p.k), self.near_in.at[side, 0], device, 12 + 2 * side)

    def far_across(self):
        p = self.p
        self.c.start(self.block(p.xf, p.oy, p.k), self.far_across_in, p.across, 17)

    def far_send(self):
        p = self.p
        self.c.arrived(self.far_across_in, 17, p.across)
        add_into(
            self.buf, self.start_of(p.xf, p.y, p.k), self.rows, self.width, 0, [self.far_across_in]
        )
        self.c.start(self.half(p.xf, p.y, p.k, 0), self.far_in.at[0], p.right, 8)
        self.c.start(self.half(p.xf, p.y, p.k, 1), self.far_in.at[1], p.left, 9)

    def near_send(self):
        p = self.p
        mid = self.width // 2
        self.c.arrived(self.far_in.at[0], 8, p.left)
        add_into(self.buf, self.start_of(p.xr, p.y, p.k), self.rows, mid, 0, [self.far_in.at[0]])
        self.c.start(self.block(p.xr, p.y, p.k), self.near_in.at[0, 1], p.right, 13)
        self.c.arrived(self.far_in.at[1], 9, p.right)
        add_into(self.buf, self.start_of(p.xl, p.y, p.k), self.rows, mid, mid, [self.far_in.at[1]])
        self.c.start(self.block(p.xl, p.y, p.k), self.near_in.at[1, 1], p.left, 15)

    def near_add(self, j):
        p = self.p
        y = (p.oy, p.y)[j]
        self.c.arrived(self.near_in.at[0, j], 12 + j, p.left)
        self.c.arrived(self.near_in.at[1, j], 14 + j, p.right)
        add_into(
            self.buf, self.start_of(p.x, y, p.k), self.rows, self.width, 0,
            [self.near_in.at[0, j], self.near_in.at[1, j]],
        )
        if j == 0:
            self.c.start(self.block(p.x, y, p.k), self.across_in, p.across, 16)

    def finish(self):
        p = self.p
        self.c.arrived(self.across_in, 16, p.across)
        add_into(
            self.buf, self.start_of(p.x, p.y, p.k), self.rows, self.width, 0, [self.across_in]
        )


def dot(a, b, dims=((1,), (0,))):
    return lax.dot_general(a, b, (dims, ((), ())), preferred_element_type=f32)


class HeadGather:
    def __init__(self, copies, buf, head, group, e):
        self.c, self.buf, self.head, self.group = copies, buf, head, group
        hi, z = lax.div(e, 4), lax.rem(e, 4)
        up, down, far = [lax.rem(z + d, 4) for d in (1, 3, 2)]
        self.e = e
        self.mirror = (1 - hi) * 4 + z
        self.up, self.down = hi * 4 + up, hi * 4 + down
        self.ups = [self.up, (1 - hi) * 4 + up]
        self.downs = [self.down, (1 - hi) * 4 + down]
        self.fars = [hi * 4 + far, (1 - hi) * 4 + far]

    def block(self, e, h, half=None):
        spot = pl.multiple_of((e * self.group + h) * self.head, 128)
        if half is None:
            return self.buf.at[:, pl.ds(spot, self.head)]
        count = self.buf.shape[0] // 2
        return self.buf.at[pl.ds(half * count, count), pl.ds(spot, self.head)]

    def own(self, h):
        mine = self.block(self.e, h)
        self.c.start(mine, mine, self.mirror, h * 9)
        self.c.start(mine, mine, self.up, h * 9 + 1)
        self.c.start(mine, mine, self.down, h * 9 + 2)

    def relay(self, h):
        got = self.block(self.mirror, h)
        self.c.arrived(got, h * 9, self.mirror)
        self.c.start(got, got, self.up, h * 9 + 3)
        self.c.start(got, got, self.down, h * 9 + 4)

    def forward(self, h):
        for i in range(2):
            self.c.arrived(self.block(self.downs[i], h), h * 9 + 1 + 2 * i, self.down)
            part = self.block(self.downs[i], h, 0)
            self.c.start(part, part, self.up, h * 9 + 5 + 2 * i)
            self.c.arrived(self.block(self.ups[i], h), h * 9 + 2 + 2 * i, self.up)
            part = self.block(self.ups[i], h, 1)
            self.c.start(part, part, self.down, h * 9 + 6 + 2 * i)

    def rest(self, h):
        for i in range(2):
            self.c.arrived(self.block(self.fars[i], h, 0), h * 9 + 5 + 2 * i, self.down)
            self.c.arrived(self.block(self.fars[i], h, 1), h * 9 + 6 + 2 * i, self.up)


class Exchange:
    def __init__(self, copies, out, into, sem, e, n):
        self.c, self.out, self.into, self.e, self.n = copies, out, into, e, n
        self.kept = pltpu.make_async_copy(out.at[e], into.at[e], sem)

    def start(self):
        for d in range(1, self.n):
            peer = lax.rem(self.e + d, self.n)
            self.c.start(self.out.at[peer], self.into.at[self.e], peer, d - 1)
        self.kept.start()

    def finish(self):
        self.kept.wait()
        for d in range(1, self.n):
            peer = lax.rem(self.e + self.n - d, self.n)
            self.c.arrived(self.into.at[peer], d - 1, peer)


def dot(a, b, dims=((1,), (0,))):
    return lax.dot_general(a, b, (dims, ((), ())), preferred_element_type=f32)


def iota(shape, axis):
    return lax.broadcasted_iota(jnp.int32, shape, axis)


def kernel(
    rows, width, hidden, head, group, n_exp,
    q_hbm, k_hbm, v_hbm, gain, routes, scores, cot_hbm, wg_hbm, wu_hbm, wd_hbm,
    mixed_out, gi_out, gg, gu, gd,
    xbuf, dybuf, wg, wu, wd, hid, dgb, dub, dhb, py, px,
    core_in, far_in, near_in, across_in, far_across_in,
    q, kv, attn, cot, slabs_out, slabs_in, spots_out, spots_in, place, mix_hi, mix_lo,
    send, recv, local_sem,
):
    p = Place()
    e = lax.axis_index("exp")
    mesh_id = pl.DeviceIdType.MESH
    tok = q.shape[0]
    tok_dev = cot.shape[0]
    slot = 8
    slots = n_exp * slot
    barrier = pltpu.get_barrier_semaphore()
    for device in (p.partner, p.across, p.right, p.left):
        pl.semaphore_signal(barrier, inc=1, device_id={"ctx": device}, device_id_type=mesh_id)
    for d in range(1, n_exp):
        pl.semaphore_signal(
            barrier, inc=1, device_id={"exp": lax.rem(e + d, n_exp)}, device_id_type=mesh_id
        )

    def copies(tensor, axis="ctx"):
        return Copies(send, recv, tensor, axis)

    gx = Gather(copies(0), xbuf, rows, width, p, True)
    gy = Gather(copies(1), dybuf, rows, width, p, True)
    ry = Reduce(copies(2), py, core_in.at[0], far_in.at[0], near_in.at[0],
                across_in.at[0], far_across_in.at[0], rows, width, p)
    rx = Reduce(copies(3), px, core_in.at[1], far_in.at[1], near_in.at[1],
                across_in.at[1], far_across_in.at[1], rows, width, p)
    gk = Gather(copies(4), kv, tok, 2 * head, p)
    ga = HeadGather(copies(5, "exp"), attn, head, group, e)
    grads_there = Exchange(copies(6, "exp"), slabs_out.at[0], slabs_in.at[0], local_sem.at[8], e, n_exp)
    spots_there = Exchange(copies(7, "exp"), spots_out, spots_in, local_sem.at[9], e, n_exp)
    y_back = Exchange(copies(8, "exp"), slabs_out.at[1], slabs_in.at[1], local_sem.at[10], e, n_exp)
    dx_back = Exchange(copies(9, "exp"), slabs_out.at[2], slabs_in.at[2], local_sem.at[11], e, n_exp)

    own = pl.ds(pl.multiple_of(((p.x * NY + p.y) * NC + p.k) * tok, 16), tok)
    first = [
        pltpu.make_async_copy(k_hbm, kv.at[own, pl.ds(0, head)], local_sem.at[0]),
        pltpu.make_async_copy(v_hbm, kv.at[own, pl.ds(head, head)], local_sem.at[1]),
        pltpu.make_async_copy(cot_hbm, cot, local_sem.at[2]),
        pltpu.make_async_copy(q_hbm, q, local_sem.at[3]),
    ]
    loads = [
        pltpu.make_async_copy(src, dst, local_sem.at[4 + i])
        for i, (src, dst) in enumerate(((wd_hbm, wd), (wg_hbm, wg), (wu_hbm, wu)))
    ]
    for copy in first + loads:
        copy.start()

    lane = iota((tok_dev, slots), 1)
    expert, order = lane >> 3, lane & 7
    in_a = routes[:, 0:1] == expert
    in_b = routes[:, 1:2] == expert
    named = jnp.where(in_a | in_b, 1.0, 0.0)
    earlier = jnp.where(iota((tok_dev, tok_dev), 1) < iota((tok_dev, tok_dev), 0), 1.0, 0.0)
    rank = dot(earlier.astype(bf16), named.astype(bf16))
    here = (named > 0.5) & (rank.astype(jnp.int32) == order)
    top = jnp.max(scores[...], axis=1, keepdims=True)
    odds_a, odds_b = jnp.exp(scores[:, 0:1] - top), jnp.exp(scores[:, 1:2] - top)
    whole = odds_a + odds_b
    mix = jnp.where(here, jnp.where(in_a, odds_a / whole, odds_b / whole), 0.0)
    placed = jnp.where(here, 1.0, 0.0).astype(bf16)
    upper = mix.astype(bf16)
    lower = (mix - upper.astype(f32)).astype(bf16)
    place[...] = placed
    mix_hi[...] = upper
    mix_lo[...] = lower
    shift = jnp.where(
        iota((tok_dev, tok), 1) == iota((tok_dev, tok), 0) + e * tok_dev, 1.0, 0.0
    ).astype(bf16)
    spots_out[...] = dot(placed, shift, ((0,), (0,))).reshape(n_exp, slot, tok)

    pl.semaphore_wait(barrier, 3 + n_exp)
    first[0].wait()
    first[1].wait()
    gk.own()
    spots_there.start()
    first[2].wait()
    chunk = 512

    @pl.loop(0, width // chunk, unroll=True)
    def _(n):
        spot = pl.ds(pl.multiple_of(n * chunk, 128), chunk)
        part = dot(mix_hi[...], cot[:, spot], ((0,), (0,))) + dot(mix_lo[...], cot[:, spot], ((0,), (0,)))
        slabs_out[0, :, :, spot] = part.reshape(n_exp, slot, chunk).astype(bf16)

    grads_there.start()
    row, from_row = iota((rows, slots), 0), iota((rows, slots), 1)
    source = (row * 43) >> 8
    squeeze = jnp.where(from_row == source * slot + (row - source * 6), 1.0, 0.0).astype(bf16)
    gk.across()
    gk.beside(0)
    gk.beside(1)
    gk.far(0)
    gk.far(1)
    spots_there.finish()
    pick = dot(squeeze, spots_in[...].reshape(slots, tok).astype(bf16)).astype(bf16)
    grads_there.finish()
    own_rows = pl.ds(pl.multiple_of(((p.x * NY + p.y) * NC + p.k) * rows, 16), rows)

    @pl.loop(0, width // chunk, unroll=True)
    def _(n):
        spot = pl.ds(pl.multiple_of(n * chunk, 128), chunk)
        slabs = slabs_in[0, :, :, spot].astype(f32).reshape(slots, chunk).astype(bf16)
        dybuf[own_rows, spot] = dot(squeeze, slabs).astype(bf16)

    gy.own()
    first[3].wait()
    for which in ("own", "left", "right", "far"):
        gk.other_core(which)
    total_keys = kv.shape[0]
    at = iota((1, total_keys), 1)
    block = at // tok
    key_pos = (((block >> 1) & 1) * NX * NC + (block >> 2) * NC + (block & 1)) * tok + at % tok
    query_pos = lax.axis_index("ctx") * tok + iota((tok, 1), 0)
    for h in range(group):
        s = dot(q[:, h * head : (h + 1) * head], kv[:, 0:head], ((1,), (1,))) * head ** (-0.5)
        s = jnp.where(key_pos <= query_pos, s, masked_value)
        weights = jnp.exp(s - jnp.max(s, axis=1, keepdims=True))
        total = jnp.sum(weights, axis=1, keepdims=True)
        out = dot(weights.astype(bf16), kv[:, head : 2 * head]) / total
        spot = pl.multiple_of((e * group + h) * head, 128)
        attn[:, pl.ds(spot, head)] = out.astype(bf16)
        ga.own(h)
    for h in range(group):
        ga.relay(h)
    gy.beside(0)
    gy.across()
    for h in range(group):
        ga.forward(h)
    for h in range(group):
        ga.rest(h)
    gy.far(0)

    def squares(n, total):
        part = attn[:, pl.ds(pl.multiple_of(n * chunk, 128), chunk)].astype(f32)
        return total + jnp.sum(part * part, axis=1, keepdims=True)

    total = lax.fori_loop(0, width // chunk, squares, jnp.zeros((tok, 1), f32), unroll=True)
    inv = lax.rsqrt(total / width + norm_eps)

    @pl.loop(0, width // chunk, unroll=True)
    def _(n):
        spot = pl.ds(pl.multiple_of(n * chunk, 128), chunk)
        normed = (attn[:, spot].astype(f32) * inv * gain[:, spot]).astype(bf16)
        xbuf[own_rows, spot] = dot(pick, normed).astype(bf16)

    gx.own()
    for copy in loads:
        copy.wait()
    col = NY * NC * rows
    tile = 256
    wtile = 512

    def back_half(x):
        at = pl.multiple_of(x * col, 16)

        @pl.loop(0, hidden // tile)
        def _(n):
            spot = pl.ds(pl.multiple_of(n * tile, 128), tile)
            dhb[pl.ds(at, col), spot] = dot(dybuf[pl.ds(at, col), :], wd[spot, :], ((1,), (1,)))

    def first_half(x):
        at = pl.multiple_of(x * col, 16)

        @pl.loop(0, hidden // tile)
        def _(n):
            cols = pl.ds(pl.multiple_of(n * tile, 128), tile)
            xs = xbuf[pl.ds(at, col), :]
            g = dot(xs, wg[:, cols])
            u = dot(xs, wu[:, cols])
            dh = dhb[pl.ds(at, col), cols]
            sig = 1.0 / (1.0 + jnp.exp(-g))
            silu = g * sig
            hid[pl.ds(at, col), cols] = (silu * u).astype(bf16)
            dub[pl.ds(at, col), cols] = (dh * silu).astype(bf16)
            dgb[pl.ds(at, col), cols] = (dh * u * sig * (1.0 + g * (1.0 - sig))).astype(bf16)

    def expert_out(x):
        at = pl.multiple_of(x * col, 16)

        @pl.loop(0, width // wtile)
        def _(n):
            spot = pl.ds(pl.multiple_of(n * wtile, 128), wtile)
            py[pl.ds(at, col), spot] = dot(hid[pl.ds(at, col), :], wd[:, spot]).astype(bf16)

    def input_grad(x):
        at = pl.multiple_of(x * col, 16)

        @pl.loop(0, width // wtile)
        def _(n):
            spot = pl.ds(pl.multiple_of(n * wtile, 128), wtile)
            px[pl.ds(at, col), spot] = (
                dot(dgb[pl.ds(at, col), :], wg[spot, :], ((1,), (1,)))
                + dot(dub[pl.ds(at, col), :], wu[spot, :], ((1,), (1,)))
            ).astype(bf16)

    def weight_grads(begin, end):
        @pl.loop(begin, end)
        def _(n):
            spot = pl.ds(pl.multiple_of(n * wtile, 128), wtile)
            gd[:, spot] = dot(hid[...], dybuf[:, spot], ((0,), (0,))).astype(bf16)
            xt = xbuf[:, spot]
            gg[spot, :] = dot(xt, dgb[...], ((0,), (0,))).astype(bf16)
            gu[spot, :] = dot(xt, dub[...], ((0,), (0,))).astype(bf16)

    def rest_of_column(which, x):
        expert_out(x)
        ry.core_send(which)
        input_grad(x)
        rx.core_send(which)

    def near_early(which):
        for work in (ry, rx):
            work.core_add(which)
            work.near_early(which - 1)

    def to_slabs(buf, which):
        row, to_row = iota((slots, rows), 1), iota((slots, rows), 0)
        source = (row * 43) >> 8
        spread = jnp.where(to_row == source * slot + (row - source * 6), 1.0, 0.0).astype(bf16)

        @pl.loop(0, width // chunk, unroll=True)
        def _(n):
            spot = pl.ds(pl.multiple_of(n * chunk, 128), chunk)
            part = dot(spread, buf[own_rows, spot])
            slabs_out[which, :, :, spot] = part.reshape(n_exp, slot, chunk).astype(bf16)

    def from_slabs(which, spot):
        return slabs_in[which, :, :, spot].astype(f32).reshape(slots, chunk).astype(bf16)

    gy.beside(1)
    gy.other_core("own")
    back_half(p.x)
    gy.other_core("right")
    gy.other_core("left")
    back_half(p.xr)
    back_half(p.xl)
    gy.far(1)
    gx.beside(0)
    gx.across()
    gx.other_core("own")
    first_half(p.x)
    rest_of_column(0, p.x)
    gx.far(0)
    gy.other_core("far")
    back_half(p.xf)
    gx.beside(1)
    gx.other_core("right")
    first_half(p.xr)
    rest_of_column(1, p.xr)
    gx.other_core("left")
    first_half(p.xl)
    near_early(1)
    rest_of_column(2, p.xl)
    gx.far(1)
    gx.other_core("far")
    first_half(p.xf)
    near_early(2)
    rest_of_column(3, p.xf)
    ry.core_add(3)
    ry.far_across()
    rx.core_add(3)
    rx.far_across()
    ry.core_add(0)
    rx.core_add(0)
    weight_grads(0, 2)
    ry.far_send()
    ry.near_add(0)
    weight_grads(2, 3)
    rx.far_send()
    rx.near_add(0)
    weight_grads(3, 4)
    ry.near_send()
    weight_grads(4, 5)
    rx.near_send()
    weight_grads(5, width // wtile)
    ry.near_add(1)
    ry.finish()
    to_slabs(py, 1)
    y_back.start()
    rx.near_add(1)
    rx.finish()
    to_slabs(px, 2)
    dx_back.start()
    y_back.finish()

    @pl.loop(0, width // chunk, unroll=True)
    def _(n):
        spot = pl.ds(pl.multiple_of(n * chunk, 128), chunk)
        slabs = from_slabs(1, spot)
        mixed_out[:, spot] = (dot(mix_hi[...], slabs) + dot(mix_lo[...], slabs)).astype(bf16)

    dx_back.finish()
    mine = pl.ds(pl.multiple_of(e * tok_dev, 16), tok_dev)
    feats = attn[mine, :].astype(f32)
    inv_own = lax.rsqrt(jnp.sum(feats * feats, axis=1, keepdims=True) / width + norm_eps)
    back = slabs_in[2].astype(f32).reshape(slots, width).astype(bf16)
    weighted = dot(place[...], back) * gain[...]
    inner = jnp.sum(weighted * feats, axis=1, keepdims=True) / width
    gi_out[...] = (inv_own * weighted - feats * (inv_own * inv_own * inv_own * inner)).astype(bf16)
    for work in (gx, gy, ry, rx, gk, ga, grads_there, spots_there, y_back, dx_back):
        work.c.drain()


def put_out(*refs):
    n = len(refs) // 2
    copies = [
        pltpu.make_async_copy(refs[i], refs[n + i], refs[-1].at[i]) for i in range(n)
    ]
    for copy in copies:
        copy.start()
    for copy in copies:
        copy.wait()


def local(queries, keys, values, norm_gain, routes, route_scores, cotangent, w_gate, w_up, w_down):
    n_exp = lax.axis_size("exp")
    head = keys.shape[1]
    group = queries.shape[1] // head
    tok = queries.shape[0]
    tok_dev, width = cotangent.shape
    rows = 3 * tok_dev
    gate_w, up_w, down_w = w_gate[0], w_up[0], w_down[0]
    hidden = gate_w.shape[1]
    total = rows * NX * NY * NC
    slots = 8 * n_exp
    hbm = pl.BlockSpec(memory_space=pl.ANY)
    vmem = pl.BlockSpec(memory_space=pltpu.VMEM)
    mixed, grad_input, grad_gate, grad_upw, grad_down = pl.pallas_call(
        functools.partial(kernel, rows, width, hidden, head, group, n_exp),
        out_shape=(
            pltpu.VMEM((tok_dev, width), bf16),
            pltpu.VMEM((tok_dev, width), bf16),
            pltpu.VMEM(gate_w.shape, bf16),
            pltpu.VMEM(up_w.shape, bf16),
            pltpu.VMEM(down_w.shape, bf16),
        ),
        in_specs=[hbm, hbm, hbm, vmem, vmem, vmem, hbm, hbm, hbm, hbm],
        out_specs=[vmem] * 5,
        scratch_shapes=[
            pltpu.VMEM((total, width), bf16),
            pltpu.VMEM((total, width), bf16),
            pltpu.VMEM(gate_w.shape, bf16),
            pltpu.VMEM(up_w.shape, bf16),
            pltpu.VMEM(down_w.shape, bf16),
            pltpu.VMEM((total, hidden), bf16),
            pltpu.VMEM((total, hidden), bf16),
            pltpu.VMEM((total, hidden), bf16),
            pltpu.VMEM((total, hidden), f32),
            pltpu.VMEM((total, width), bf16),
            pltpu.VMEM((total, width), bf16),
            pltpu.VMEM((2, 4, 2, rows, width), bf16),
            pltpu.VMEM((2, 2, rows, width // 2), bf16),
            pltpu.VMEM((2, 2, 2, rows, width), bf16),
            pltpu.VMEM((2, rows, width), bf16),
            pltpu.VMEM((2, rows, width), bf16),
            pltpu.VMEM(queries.shape, bf16),
            pltpu.VMEM((tok * NX * NY * NC, 2 * head), bf16),
            pltpu.VMEM((tok, width), bf16),
            pltpu.VMEM((tok_dev, width), bf16),
            pltpu.VMEM((3, n_exp, 8, width), bf16),
            pltpu.VMEM((3, n_exp, 8, width), bf16),
            pltpu.VMEM((n_exp, 8, tok), f32),
            pltpu.VMEM((n_exp, 8, tok), f32),
            pltpu.VMEM((tok_dev, slots), bf16),
            pltpu.VMEM((tok_dev, slots), bf16),
            pltpu.VMEM((tok_dev, slots), bf16),
            pltpu.SemaphoreType.DMA((10, 27)),
            pltpu.SemaphoreType.DMA((10, 27)),
            pltpu.SemaphoreType.DMA((12,)),
        ],
        compiler_params=pltpu.CompilerParams(
            collective_id=0, has_side_effects=True, vmem_limit_bytes=54000000
        ),
        name="layer",
    )(
        queries, keys, values, norm_gain.reshape(1, width), routes, route_scores, cotangent,
        gate_w, up_w, down_w,
    )
    results = (mixed, grad_input, grad_gate, grad_upw, grad_down)
    mixed, grad_input, grad_gate, grad_upw, grad_down = pl.pallas_call(
        put_out,
        out_shape=tuple(jax.ShapeDtypeStruct(r.shape, r.dtype) for r in results),
        in_specs=[hbm] * 5,
        out_specs=[hbm] * 5,
        scratch_shapes=[pltpu.SemaphoreType.DMA((5,))],
        compiler_params=pltpu.CompilerParams(vmem_limit_bytes=1000000),
        name="put_out",
    )(*results)
    return (mixed, grad_input, grad_gate[None], grad_upw[None], grad_down[None])


def solution(mesh):
    placed = (
        P("ctx", "exp"),
        P("ctx", "exp"),
        P("ctx", "exp"),
        P(),
        P(("ctx", "exp"), None),
        P(("ctx", "exp"), None),
        P(("ctx", "exp"), None),
        P("exp", None, "ctx"),
        P("exp", None, "ctx"),
        P("exp", "ctx", None),
    )
    return jax.shard_map(
        local,
        mesh=mesh,
        in_specs=placed,
        out_specs=(
            P(("ctx", "exp"), None),
            P(("ctx", "exp"), None),
            P("exp", None, "ctx"),
            P("exp", None, "ctx"),
            P("exp", "ctx", None),
        ),
        check_vma=False,
    )
```
